256 devices in a mesh: tm: 128 (over y, x, z), space: 2 (over core).
Axes of the slice: x: 4, y: 4, z: 8, core: 2. Of those that a mesh axis runs over, the one named last changes fastest.
Arguments:
- forcing: float32 [128, 512, 8, 256], P('tm', None, None, 'space'), may hold values from -6 to 6
- initial: float32 [512, 64, 256], P('tm', None, 'space'), may hold values from -6 to 6
- diffusion: float32 [512, 64, 256], P('tm', None, 'space'), may hold values from 0.25 to 4
- drift: float32 [512, 64, 256], P('tm', None, 'space'), may hold values from 0.2 to 1.5
Outputs:
- states: float32 [128, 512, 8, 256], P('tm', None, None, 'space')
The draws below stay inside these ranges and needn't reach their ends.
All inputs are finite; a program needn't handle non-finite values.
Results may differ from the reference program's by a relative error of at most 0.00002.
Values sent between devices are 32-bit elements; how exact they have to be, the bound alone decides.
A program may use at most 64 MiB of HBM per device.

```python
import math
import jax
import jax.numpy as jnp
from jax import lax

NT = 16
NX = 64
SWEEPS = 4
XS = 8
NZ = 512
NY = 256


def steps_of(own_key, dims, cuts, smallest, high):
    loudness = 1.0
    for position, blocks in cuts:
        steps = jax.random.uniform(jax.random.fold_in(jax.random.fold_in(own_key, 6), position), (blocks,), jnp.float32, smallest / len(cuts), high / len(cuts))
        loudness = loudness * jnp.repeat(jnp.exp(steps), dims[position] // blocks).reshape((-1,) + (1,) * (len(dims) - 1 - position))
    return loudness


def noise(own_key, shape, spread, reach, pieces=(), dtype=jnp.bfloat16):
    loudness = steps_of(own_key, shape, pieces, -0.22, 0.18) if pieces else 1.0
    drawn = jax.random.normal(own_key, shape, jnp.float32) * spread * loudness
    return jnp.minimum(jnp.maximum(drawn, -reach), reach).astype(dtype)


def setup_inputs(seed: int = 0) -> dict:
    arg_keys = jax.random.split(jax.random.key(seed), 5)
    return {
        "forcing": noise(arg_keys[0], (NT * XS, NZ, NX // XS, NY), 1.0, 6.0, ((0, 128), (3, 2)), jnp.float32),
        "initial": noise(arg_keys[1], (NZ, NX, NY), 1.0, 6.0, ((0, 128), (2, 2)), jnp.float32),
        "diffusion": jnp.clip(jnp.exp(math.log(4.0) - 2.7725887 * jax.random.uniform(arg_keys[2], (NZ, NX, NY), jnp.float32) ** steps_of(arg_keys[2], (NZ, NX, NY), ((0, 128), (2, 2)), -0.2, 0.2)), 0.25, 4.0),
        "drift": jnp.clip(0.2 + 1.3 * jax.random.uniform(arg_keys[3], (NZ, NX, NY), jnp.float32) ** steps_of(arg_keys[3], (NZ, NX, NY), ((0, 128), (2, 2)), -0.2, 0.2), 0.2, 1.5),
    }


def relax_cells(field, source, diffus, drift_rate):
    widened = jnp.pad(field, ((0, 0), (1, 1), (0, 0)))
    beside = field[2:, :, 1:-1] + field[:-2, :, 1:-1]
    beside = beside + field[1:-1, :, 2:] + field[1:-1, :, :-2]
    beside = beside + widened[1:-1, 2:, 1:-1] + widened[1:-1, :-2, 1:-1]
    upstream = field[:-2, :, 1:-1]
    return (source + diffus * beside + drift_rate * upstream) / (1.0 + 6.0 * diffus + drift_rate)


def reference(forcing, initial, diffusion, drift):
    nzall = forcing.shape[1]
    xpart = forcing.shape[2]
    nyall = forcing.shape[3]
    force = forcing.reshape(NT, XS, nzall, xpart, nyall).transpose(0, 2, 1, 3, 4)
    force = force.reshape(NT, nzall, XS * xpart, nyall)

    def advance(current, forcing_now):
        source = current + forcing_now
        field = current
        for sweep_index in range(SWEEPS):
            padded = jnp.pad(field, ((1, 1), (0, 0), (1, 1)))
            field = relax_cells(padded, source, diffusion, drift)
        return field, field

    final, result = lax.scan(advance, initial, force)
    result = result.reshape(NT, nzall, XS, xpart, nyall).transpose(0, 2, 1, 3, 4)
    return result.reshape(NT * XS, nzall, xpart, nyall)
```

```python
import jax
import jax.numpy as jnp
from jax import lax
from jax.experimental import pallas as pl
from jax.experimental.pallas import tpu as pltpu
from jax.sharding import PartitionSpec as P

NT = 16
COLS = 16
RING = 8
LEAD = 6
MESH = pl.DeviceIdType.MESH
F32 = jnp.float32


def remote(src, dst, send, recv, device):
    return pltpu.make_async_remote_copy(
        src_ref=src, dst_ref=dst, send_sem=send, recv_sem=recv, device_id=device, device_id_type=MESH
    )


def await_bytes(ref, sem):
    pltpu.make_async_copy(ref, ref, sem).wait()


def kernel(
    forcing, initial, diffusion, drift, out,
    F, G, O, E, C, D, R, DP, EP, IV, SP, W1, W2,
    csend, crecv, xsend, xrecv, fsend, frecv, gsend, grecv, hsend, hrecv, osend, orecv,
):
    t = lax.axis_index("tm")
    c = lax.axis_index("space")
    q = t // RING
    j = t % RING
    part = 2 * q + c

    def plane_device(p):
        return ((p // 2) * RING + j, p % 2)

    barrier = pltpu.get_barrier_semaphore()

    def greet(device):
        pl.semaphore_signal(barrier, inc=1, device_id=device, device_id_type=MESH)

    @pl.loop(1, 2 * COLS)
    def _(n):
        greet(plane_device((part + n) % (2 * COLS)))

    @pl.loop(1, RING)
    def _(n):
        chip = q * RING + (j + n) % RING
        greet((chip, c))
        greet((chip, 1 - c))

    beyond = (q + COLS - 1 + 2 * c) % COLS
    left, right = (j + RING - 1) % RING, (j + 1) % RING
    greet((beyond * RING + left, 1 - c))
    greet((beyond * RING + right, 1 - c))
    pl.semaphore_wait(barrier, (2 * COLS - 1) + 2 * (RING - 1) + 2)

    up = (part + 1) % (2 * COLS)
    down = (part + 2 * COLS - 1) % (2 * COLS)

    def at(p, jj):
        return ((p // 2) * RING + jj, p % 2)

    lower = pl.ds(4, 4)
    upper = pl.ds(0, 4)

    def halo_copies(A, send, recv):
        lo, hi = pl.ds(4, 4), pl.ds(16, 4)
        own = pl.ds(4, 16)
        below, above = pl.ds(0, 4), pl.ds(20, 4)
        moves = [
            (own, 0, lower, own, 1, part, left),
            (own, 1, upper, own, 0, part, right),
            (hi, 0, lower, below, 1, up, left),
            (hi, 1, upper, below, 0, up, right),
            (lo, 0, lower, above, 1, down, left),
            (lo, 1, upper, above, 0, down, right),
            (hi, 0, lower, below, 0, up, j),
            (hi, 1, upper, below, 1, up, j),
            (lo, 0, lower, above, 0, down, j),
            (lo, 1, upper, above, 1, down, j),
        ]
        for zs, tile, rows, zd, tiled, p, jj in moves:
            remote(
                A.at[zs, tile, :, rows, :], A.at[zd, tiled, :, rows, :], send, recv, at(p, jj)
            ).start()

    half = j // 4
    zs = pl.ds((j % 4) * 4, 4)
    stay = c == half
    for n in range(RING):
        jj = (j + n) % RING
        for a, ref in enumerate((initial, diffusion, drift)):
            src = ref.at[:, pl.ds(pl.multiple_of(jj * 8, 8), 8), :]
            dst = C.at[a, c, zs]
            if n == 0:
                @pl.when(stay)
                def _():
                    pltpu.make_async_copy(src, dst, crecv).start()

                @pl.when(jnp.logical_not(stay))
                def _():
                    remote(src, dst, csend, crecv, (t, 1 - c)).start()
            else:
                remote(src, dst, csend, crecv, (q * RING + jj, half)).start()

    def send_forcing(first, last):
        @pl.loop(first, last)
        def _(n):
            p = (part + n) % (2 * COLS)
            remote(
                forcing.at[0, pl.ds(p * 16, 16)], F.at[2 * q + c], fsend, frecv.at[q], plane_device(p)
            ).start()

    def keep_forcing():
        pltpu.make_async_copy(forcing.at[0, pl.ds(part * 16, 16)], F.at[2 * q + c], frecv.at[q]).start()

    @pl.when(q < LEAD)
    def _():
        keep_forcing()
        send_forcing(1, 2 * COLS)

    def place(A, h, v):
        A[pl.ds(4, 16), 0, h, pl.ds(4, 4), :] = v[:, 0:4, :]
        A[pl.ds(4, 16), 1, h, pl.ds(0, 4), :] = v[:, 4:8, :]

    await_bytes(C, crecv)
    for h in range(2):
        place(D, h, C[1, h])
        place(R, h, C[2, h])
    halo_copies(D, xsend, xrecv)
    halo_copies(R, xsend, xrecv)
    for h in range(2):
        place(E.at[0], h, C[0, h])
    halo_copies(E.at[0], hsend.at[0], hrecv.at[0])

    def prepare_force(k):
        await_bytes(F.at[pl.ds(2 * k, 2)], frecv.at[k])
        for h in range(2):
            place(G.at[k], h, F[2 * k + h])
        halo_copies(G.at[k], gsend, grecv.at[k])

    def clear_outside(A):
        @pl.when(part == 0)
        def _():
            A[pl.ds(0, 4)] = jnp.zeros((4, 2, 2, 8, 128), F32)

        @pl.when(part == 2 * COLS - 1)
        def _():
            A[pl.ds(20, 4)] = jnp.zeros((4, 2, 2, 8, 128), F32)

        @pl.when(j == 0)
        def _():
            A[:, 0, :, pl.ds(0, 4), :] = jnp.zeros((24, 2, 4, 128), F32)

        @pl.when(j == RING - 1)
        def _():
            A[:, 1, :, pl.ds(4, 4), :] = jnp.zeros((24, 2, 4, 128), F32)

    await_bytes(G.at[pl.ds(0, 2), pl.ds(0, 16)], xrecv)
    for z in range(0, 24, 4):
        s = pl.ds(z, 4)
        d, r = D[s], R[s]
        inv = 1.0 / (1.0 + 6.0 * d + r)
        IV[s] = inv
        DP[s] = d * inv
        EP[s] = (d + r) * inv
    for A in (IV, DP, EP):
        clear_outside(A)

    prepare_force(0)
    prepare_force(1)

    def relax(load, load_s, z, n):
        shape = (n, 8, 128)
        row = lax.broadcasted_iota(jnp.int32, shape, 1)
        lane = lax.broadcasted_iota(jnp.int32, shape, 2)
        first_row, last_row = row == 0, row == 7
        first_lane, last_lane = lane == 0, lane == 127
        zero = jnp.zeros(shape, F32)
        wide = [[load(z - 1, n + 2, T, h) for h in range(2)] for T in range(2)]
        mid = [[wide[T][h][1:-1] for h in range(2)] for T in range(2)]
        result = [[None, None], [None, None]]
        beside = [[None, None], [None, None]]
        for h in range(2):
            a0, a1 = pltpu.roll(mid[0][h], 1, 1), pltpu.roll(mid[1][h], 1, 1)
            b0, b1 = pltpu.roll(mid[0][h], 7, 1), pltpu.roll(mid[1][h], 7, 1)
            beside[0][h] = a0 + jnp.where(last_row, b1, b0)
            beside[1][h] = jnp.where(first_row, a0, a1) + b1
        for T in range(2):
            a0, a1 = pltpu.roll(mid[T][0], 1, 2), pltpu.roll(mid[T][1], 1, 2)
            b0, b1 = pltpu.roll(mid[T][0], 127, 2), pltpu.roll(mid[T][1], 127, 2)
            across = (
                jnp.where(first_lane, zero, a0) + jnp.where(last_lane, b1, b0),
                jnp.where(first_lane, a0, a1) + jnp.where(last_lane, zero, b1),
            )
            for h in range(2):
                total = beside[T][h] + across[h] + wide[T][h][2:]
                s = pl.ds(z, n)
                result[T][h] = (
                    load_s(z, n, T, h) + DP[s, T, h] * total + EP[s, T, h] * wide[T][h][:-2]
                )
        return result

    def chunks(first, last):
        z = first
        while z < last:
            n = min(4, last - z)
            yield z, n
            z += n

    def from_ref(A):
        return lambda z, n, T, h: A[pl.ds(z, n), T, h]

    @pl.loop(0, NT)
    def _(k):
        par = k % 2
        now, later = E.at[par], E.at[1 - par]
        force = G.at[k]
        await_bytes(G.at[0, pl.ds(0, 16)], hrecv.at[par])
        await_bytes(G.at[0, pl.ds(0, 16)], grecv.at[k])
        clear_outside(now)

        def make_source(z, n, T, h):
            s = pl.ds(z, n)
            v = (now[s, T, h] + force[s, T, h]) * IV[s, T, h]
            SP[s, T, h] = v
            return v

        for load, load_s, W, margin in (
            (from_ref(now), make_source, W1, 1),
            (from_ref(W1), from_ref(SP), W2, 2),
            (from_ref(W2), from_ref(SP), W1, 3),
        ):
            for z, n in chunks(margin, 24 - margin):
                v = relax(load, load_s, z, n)
                for T in range(2):
                    for h in range(2):
                        W[pl.ds(z, n), T, h] = v[T][h]

        @pl.when(k > 0)
        def _():
            await_bytes(G.at[0, pl.ds(0, 16)], hsend.at[1 - par])

        for z, n in chunks(4, 20):
            v = relax(from_ref(W1), from_ref(SP), z, n)
            row = lax.broadcasted_iota(jnp.int32, (n, 8, 128), 1)
            for h in range(2):
                later[pl.ds(z, n), 0, h, pl.ds(4, 4), :] = v[0][h][:, 4:8, :]
                later[pl.ds(z, n), 1, h, pl.ds(0, 4), :] = v[1][h][:, 0:4, :]
                O[k, h, pl.ds(z - 4, n)] = jnp.where(
                    row < 4, pltpu.roll(v[0][h], 4, 1), pltpu.roll(v[1][h], 4, 1)
                )

        @pl.when(k < NT - 1)
        def _():
            halo_copies(later, hsend.at[1 - par], hrecv.at[1 - par])

        for h in range(2):
            src, dst = O.at[k, h], out.at[0, pl.ds(part * 16, 16)]
            mine = jnp.logical_and(k == q, c == h)

            @pl.when(mine)
            def _():
                pltpu.make_async_copy(src, dst, orecv).start()

            @pl.when(jnp.logical_not(mine))
            def _():
                remote(src, dst, osend, orecv, (k * RING + j, h)).start()

        @pl.when(q - LEAD == k)
        def _():
            keep_forcing()
            send_forcing(1, COLS)

        @pl.when(q - LEAD + 1 == k)
        def _():
            @pl.when(q >= LEAD)
            def _():
                send_forcing(COLS, 2 * COLS)

        @pl.when(k < NT - 2)
        def _():
            prepare_force(k + 2)

    @pl.when(stay)
    def _():
        await_bytes(F.at[pl.ds(0, 6), pl.ds(0, 14)], csend)

    @pl.when(jnp.logical_not(stay))
    def _():
        await_bytes(C, csend)

    await_bytes(G.at[pl.ds(0, 2), pl.ds(0, 16)], xsend)
    await_bytes(G.at[0, pl.ds(0, 16)], hsend.at[1])
    await_bytes(G.at[:, pl.ds(0, 16)], gsend)
    await_bytes(F.at[pl.ds(0, 31)], fsend)
    await_bytes(F.at[pl.ds(0, 31)], osend)
    await_bytes(out, orecv)


def per_device(forcing, initial, diffusion, drift):
    wide = (24, 2, 2, 8, 128)
    vmem = lambda *shape: pltpu.VMEM(shape, F32)
    dma = pltpu.SemaphoreType.DMA
    return pl.pallas_call(
        kernel,
        out_shape=jax.ShapeDtypeStruct(forcing.shape, F32),
        in_specs=[pl.BlockSpec(memory_space=pl.ANY)] * 4,
        out_specs=pl.BlockSpec(memory_space=pl.ANY),
        scratch_shapes=[
            vmem(2 * NT, 16, 8, 128),
            vmem(NT, *wide),
            vmem(NT, 2, 16, 8, 128),
            vmem(2, *wide),
            vmem(3, 2, 16, 8, 128),
        ]
        + [vmem(*wide)] * 8
        + [dma, dma, dma, dma, dma, dma((NT,)), dma, dma((NT,)), dma((2,)), dma((2,)), dma, dma],
        compiler_params=pltpu.CompilerParams(
            collective_id=0, has_side_effects=True, vmem_limit_bytes=40 * 1024 * 1024
        ),
    )(forcing, initial, diffusion, drift)


def solution(mesh):
    in_specs = (
        P("tm", None, None, "space"),
        P("tm", None, "space"),
        P("tm", None, "space"),
        P("tm", None, "space"),
    )
    out_specs = P("tm", None, None, "space")
    return jax.shard_map(
        per_device, mesh=mesh, in_specs=in_specs, out_specs=out_specs, check_vma=False
    )
```

```python
import jax
import jax.numpy as jnp
from jax import lax
from jax.experimental import pallas as pl
from jax.experimental.pallas import tpu as pltpu
from jax.sharding import PartitionSpec as P

NT = 16
COLS = 16
RING = 8
LEAD = 6
MESH = pl.DeviceIdType.MESH
F32 = jnp.float32


def snake(n):
    y, x = n // 4, n % 4
    return y * 4 + x + (y % 2) * (3 - 2 * x)


def remote(src, dst, send, recv, device):
    return pltpu.make_async_remote_copy(
        src_ref=src, dst_ref=dst, send_sem=send, recv_sem=recv, device_id=device, device_id_type=MESH
    )


def await_bytes(ref, sem):
    pltpu.make_async_copy(ref, ref, sem).wait()


def kernel(
    forcing, initial, diffusion, drift, out,
    F, G, O, E, C, D, R, DP, EP, IV, SP, W1, W2,
    csend, crecv, xsend, xrecv, fsend, frecv, gsend, grecv, hsend, hrecv, osend, orecv,
):
    t = lax.axis_index("tm")
    c = lax.axis_index("space")
    q = t // RING
    j = t % RING
    part = 2 * snake(q) + c

    def at(p, jj):
        return (snake(p // 2) * RING + jj, p % 2)

    def plane_device(p):
        return at(p, j)

    barrier = pltpu.get_barrier_semaphore()

    def greet(device):
        pl.semaphore_signal(barrier, inc=1, device_id=device, device_id_type=MESH)

    @pl.loop(1, 2 * COLS)
    def _(n):
        greet(plane_device((part + n) % (2 * COLS)))

    @pl.loop(1, RING)
    def _(n):
        chip = snake(q) * RING + (j + n) % RING
        greet((chip, c))
        greet((chip, 1 - c))

    left, right = (j + RING - 1) % RING, (j + 1) % RING
    up = (part + 1) % (2 * COLS)
    down = (part + 2 * COLS - 1) % (2 * COLS)
    for jj in (left, right):
        for p in (part, up, down):
            greet(at(p, jj))
    pl.semaphore_wait(barrier, (2 * COLS - 1) + 2 * (RING - 1) + 6)

    has_left, has_right = j > 0, j < RING - 1
    has_down, has_up = part > 0, part < 2 * COLS - 1
    x_edge = jnp.logical_or(j == 0, j == RING - 1)
    z_edge = jnp.logical_or(part == 0, part == 2 * COLS - 1)

    lower = pl.ds(4, 4)
    upper = pl.ds(0, 4)

    def halo_copies(A, send, recv):
        lo, hi = pl.ds(4, 4), pl.ds(16, 4)
        own = pl.ds(4, 16)
        below, above = pl.ds(0, 4), pl.ds(20, 4)

        def move(zs, tile, rows, zd, tiled, p, jj, group):
            remote(
                A.at[zs, tile, :, rows, :], A.at[zd, tiled, :, rows, :],
                send.at[group], recv.at[group], at(p, jj),
            ).start()

        for has_z, zs, zd, p in ((has_up, hi, below, up), (has_down, lo, above, down)):
            @pl.when(jnp.logical_and(has_z, has_left))
            def _():
                move(zs, 0, lower, zd, 1, p, left, 2)

            @pl.when(jnp.logical_and(has_z, has_right))
            def _():
                move(zs, 1, upper, zd, 0, p, right, 2)

        @pl.when(has_left)
        def _():
            move(own, 0, lower, own, 1, part, left, 0)

        @pl.when(has_right)
        def _():
            move(own, 1, upper, own, 0, part, right, 0)

        for has_z, zs, zd, p in ((has_up, hi, below, up), (has_down, lo, above, down)):
            @pl.when(has_z)
            def _():
                move(zs, 0, lower, zd, 0, p, j, 1)
                move(zs, 1, upper, zd, 1, p, j, 1)

    def await_halos(sem):
        inside = jnp.logical_not

        def await_tiles(condition, group, n):
            @pl.when(condition)
            def _():
                await_bytes(G.at[0, pl.ds(0, n // 4)], sem.at[group])

        await_tiles(inside(x_edge), 0, 32)
        await_tiles(x_edge, 0, 16)
        await_tiles(inside(z_edge), 1, 16)
        await_tiles(z_edge, 1, 8)
        await_tiles(jnp.logical_and(inside(z_edge), inside(x_edge)), 2, 16)
        await_tiles(jnp.logical_and(z_edge, inside(x_edge)), 2, 8)
        await_tiles(jnp.logical_and(inside(z_edge), x_edge), 2, 8)
        await_tiles(jnp.logical_and(z_edge, x_edge), 2, 4)

    half = j // 4
    zs = pl.ds((j % 4) * 4, 4)
    home = snake(q) == q
    stay = jnp.logical_and(c == half, home)
    for n in range(RING):
        jj = (j + n) % RING
        for a, ref in enumerate((initial, diffusion, drift)):
            src = ref.at[:, pl.ds(pl.multiple_of(jj * 8, 8), 8), :]
            dst = C.at[a, c, zs]
            if n == 0:
                @pl.when(stay)
                def _():
                    pltpu.make_async_copy(src, dst, crecv).start()

                @pl.when(jnp.logical_not(stay))
                def _():
                    remote(src, dst, csend, crecv, (snake(q) * RING + j, half)).start()
            else:
                remote(src, dst, csend, crecv, (snake(q) * RING + jj, half)).start()

    def send_forcing(first, last):
        @pl.loop(first, last)
        def _(n):
            p = (part + n) % (2 * COLS)
            remote(
                forcing.at[0, pl.ds(p * 16, 16)], F.at[2 * q + c], fsend, frecv.at[q], plane_device(p)
            ).start()

    def keep_forcing():
        pltpu.make_async_copy(forcing.at[0, pl.ds(part * 16, 16)], F.at[2 * q + c], frecv.at[q]).start()

    @pl.when(q < LEAD)
    def _():
        keep_forcing()
        send_forcing(1, 2 * COLS)

    def place(A, h, v):
        A[pl.ds(4, 16), 0, h, pl.ds(4, 4), :] = v[:, 0:4, :]
        A[pl.ds(4, 16), 1, h, pl.ds(0, 4), :] = v[:, 4:8, :]

    def clear_outside(A):
        @pl.when(part == 0)
        def _():
            A[pl.ds(0, 4)] = jnp.zeros((4, 2, 2, 8, 128), F32)

        @pl.when(part == 2 * COLS - 1)
        def _():
            A[pl.ds(20, 4)] = jnp.zeros((4, 2, 2, 8, 128), F32)

        @pl.when(j == 0)
        def _():
            A[:, 0, :, pl.ds(0, 4), :] = jnp.zeros((24, 2, 4, 128), F32)

        @pl.when(j == RING - 1)
        def _():
            A[:, 1, :, pl.ds(4, 4), :] = jnp.zeros((24, 2, 4, 128), F32)

    clear_outside(E.at[0])
    clear_outside(E.at[1])
    await_bytes(C, crecv)
    for h in range(2):
        place(D, h, C[1, h])
        place(R, h, C[2, h])
    halo_copies(D, xsend.at[0], xrecv.at[0])
    halo_copies(R, xsend.at[1], xrecv.at[1])
    for h in range(2):
        place(E.at[0], h, C[0, h])
    halo_copies(E.at[0], hsend.at[0], hrecv.at[0])

    def prepare_force(k):
        await_bytes(F.at[pl.ds(2 * k, 2)], frecv.at[k])
        clear_outside(G.at[k])
        for h in range(2):
            place(G.at[k], h, F[2 * k + h])
        halo_copies(G.at[k], gsend.at[k], grecv.at[k])

    await_halos(xrecv.at[0])
    await_halos(xrecv.at[1])
    for z in range(0, 24, 4):
        s = pl.ds(z, 4)
        d, r = D[s], R[s]
        inv = 1.0 / (1.0 + 6.0 * d + r)
        IV[s] = inv
        DP[s] = d * inv
        EP[s] = (d + r) * inv
    for A in (IV, DP, EP):
        clear_outside(A)

    prepare_force(0)
    prepare_force(1)

    def relax(load, load_s, z, n):
        shape = (n, 8, 128)
        row = lax.broadcasted_iota(jnp.int32, shape, 1)
        lane = lax.broadcasted_iota(jnp.int32, shape, 2)
        first_row, last_row = row == 0, row == 7
        first_lane, last_lane = lane == 0, lane == 127
        zero = jnp.zeros(shape, F32)
        wide = [[load(z - 1, n + 2, T, h) for h in range(2)] for T in range(2)]
        mid = [[wide[T][h][1:-1] for h in range(2)] for T in range(2)]
        result = [[None, None], [None, None]]
        beside = [[None, None], [None, None]]
        for h in range(2):
            a0, a1 = pltpu.roll(mid[0][h], 1, 1), pltpu.roll(mid[1][h], 1, 1)
            b0, b1 = pltpu.roll(mid[0][h], 7, 1), pltpu.roll(mid[1][h], 7, 1)
            beside[0][h] = a0 + jnp.where(last_row, b1, b0)
            beside[1][h] = jnp.where(first_row, a0, a1) + b1
        for T in range(2):
            a0, a1 = pltpu.roll(mid[T][0], 1, 2), pltpu.roll(mid[T][1], 1, 2)
            b0, b1 = pltpu.roll(mid[T][0], 127, 2), pltpu.roll(mid[T][1], 127, 2)
            across = (
                jnp.where(first_lane, zero, a0) + jnp.where(last_lane, b1, b0),
                jnp.where(first_lane, a0, a1) + jnp.where(last_lane, zero, b1),
            )
            for h in range(2):
                total = beside[T][h] + across[h] + wide[T][h][2:]
                s = pl.ds(z, n)
                result[T][h] = (
                    load_s(z, n, T, h) + DP[s, T, h] * total + EP[s, T, h] * wide[T][h][:-2]
                )
        return result

    def chunks(first, last):
        z = first
        while z < last:
            n = min(4, last - z)
            yield z, n
            z += n

    def from_ref(A):
        return lambda z, n, T, h: A[pl.ds(z, n), T, h]

    @pl.loop(0, NT)
    def _(k):
        par = k % 2
        now, later = E.at[par], E.at[1 - par]
        force = G.at[k]
        await_halos(hrecv.at[par])
        await_halos(grecv.at[k])

        def make_source(z, n, T, h):
            s = pl.ds(z, n)
            v = (now[s, T, h] + force[s, T, h]) * IV[s, T, h]
            SP[s, T, h] = v
            return v

        for load, load_s, W, margin in (
            (from_ref(now), make_source, W1, 1),
            (from_ref(W1), from_ref(SP), W2, 2),
            (from_ref(W2), from_ref(SP), W1, 3),
        ):
            for z, n in chunks(margin, 24 - margin):
                v = relax(load, load_s, z, n)
                for T in range(2):
                    for h in range(2):
                        W[pl.ds(z, n), T, h] = v[T][h]

        @pl.when(k > 0)
        def _():
            await_halos(hsend.at[1 - par])

        for z, n in chunks(4, 20):
            v = relax(from_ref(W1), from_ref(SP), z, n)
            row = lax.broadcasted_iota(jnp.int32, (n, 8, 128), 1)
            for h in range(2):
                later[pl.ds(z, n), 0, h, pl.ds(4, 4), :] = v[0][h][:, 4:8, :]
                later[pl.ds(z, n), 1, h, pl.ds(0, 4), :] = v[1][h][:, 0:4, :]
                O[k, h, pl.ds(z - 4, n)] = jnp.where(
                    row < 4, pltpu.roll(v[0][h], 4, 1), pltpu.roll(v[1][h], 4, 1)
                )

        @pl.when(k < NT - 1)
        def _():
            halo_copies(later, hsend.at[1 - par], hrecv.at[1 - par])

        for h in range(2):
            src, dst = O.at[k, h], out.at[0, pl.ds(part * 16, 16)]
            mine = jnp.logical_and(k == q, c == h)

            @pl.when(mine)
            def _():
                pltpu.make_async_copy(src, dst, orecv).start()

            @pl.when(jnp.logical_not(mine))
            def _():
                remote(src, dst, osend, orecv, (k * RING + j, h)).start()

        @pl.when(q - LEAD == k)
        def _():
            keep_forcing()
            send_forcing(1, COLS)

        @pl.when(q - LEAD + 1 == k)
        def _():
            @pl.when(q >= LEAD)
            def _():
                send_forcing(COLS, 2 * COLS)

        @pl.when(k < NT - 2)
        def _():
            prepare_force(k + 2)

    @pl.when(stay)
    def _():
        await_bytes(F.at[pl.ds(0, 6), pl.ds(0, 14)], csend)

    @pl.when(jnp.logical_not(stay))
    def _():
        await_bytes(C, csend)

    await_halos(xsend.at[0])
    await_halos(xsend.at[1])
    await_halos(hsend.at[1])

    @pl.loop(0, NT)
    def _(k):
        await_halos(gsend.at[k])

    await_bytes(F.at[pl.ds(0, 31)], fsend)
    await_bytes(F.at[pl.ds(0, 31)], osend)
    await_bytes(out, orecv)


def per_device(forcing, initial, diffusion, drift):
    wide = (24, 2, 2, 8, 128)
    vmem = lambda *shape: pltpu.VMEM(shape, F32)
    dma = pltpu.SemaphoreType.DMA
    return pl.pallas_call(
        kernel,
        out_shape=jax.ShapeDtypeStruct(forcing.shape, F32),
        in_specs=[pl.BlockSpec(memory_space=pltpu.HBM)] * 4,
        out_specs=pl.BlockSpec(memory_space=pl.ANY),
        scratch_shapes=[
            vmem(2 * NT, 16, 8, 128),
            vmem(NT, *wide),
            vmem(NT, 2, 16, 8, 128),
            vmem(2, *wide),
            vmem(3, 2, 16, 8, 128),
        ]
        + [vmem(*wide)] * 8
        + [dma, dma, dma((2, 3)), dma((2, 3)), dma, dma((NT,)), dma((NT, 3)), dma((NT, 3))]
        + [dma((2, 3)), dma((2, 3)), dma, dma],
        compiler_params=pltpu.CompilerParams(
            collective_id=0, has_side_effects=True, vmem_limit_bytes=60 * 1024 * 1024
        ),
    )(forcing, initial, diffusion, drift)


def solution(mesh):
    in_specs = (
        P("tm", None, None, "space"),
        P("tm", None, "space"),
        P("tm", None, "space"),
        P("tm", None, "space"),
    )
    out_specs = P("tm", None, None, "space")
    return jax.shard_map(
        per_device, mesh=mesh, in_specs=in_specs, out_specs=out_specs, check_vma=False
    )
```

```python
import jax
import jax.numpy as jnp
from jax import lax
from jax.experimental import pallas as pl
from jax.experimental.pallas import tpu as pltpu
from jax.sharding import PartitionSpec as P

NT = 16
COLS = 16
RING = 8
FIRST = 3
PIECES = 4
MESH = pl.DeviceIdType.MESH
F32 = jnp.float32


def snake(n):
    y, x = n // 4, n % 4
    return y * 4 + x + (y % 2) * (3 - 2 * x)


def remote(src, dst, send, recv, device):
    return pltpu.make_async_remote_copy(
        src_ref=src, dst_ref=dst, send_sem=send, recv_sem=recv, device_id=device, device_id_type=MESH
    )


def await_bytes(ref, sem):
    pltpu.make_async_copy(ref, ref, sem).wait()


def kernel(
    forcing, initial, diffusion, drift, out,
    F, G, O, E, C, D, R, DP, EP, IV, SP, W1, W2,
    csend, crecv, xsend, xrecv, fsend, frecv, gsend, grecv, hsend, hrecv, osend, orecv,
):
    t = lax.axis_index("tm")
    c = lax.axis_index("space")
    q = t // RING
    j = t % RING
    part = 2 * snake(q) + c

    def at(p, jj):
        return (snake(p // 2) * RING + jj, p % 2)

    def plane_device(p):
        return at(p, j)

    barrier = pltpu.get_barrier_semaphore()

    def greet(device):
        pl.semaphore_signal(barrier, inc=1, device_id=device, device_id_type=MESH)

    @pl.loop(1, 2 * COLS)
    def _(n):
        greet(plane_device((part + n) % (2 * COLS)))

    @pl.loop(1, RING)
    def _(n):
        chip = snake(q) * RING + (j + n) % RING
        greet((chip, c))
        greet((chip, 1 - c))

    left, right = (j + RING - 1) % RING, (j + 1) % RING
    up = (part + 1) % (2 * COLS)
    down = (part + 2 * COLS - 1) % (2 * COLS)
    for jj in (left, right):
        for p in (part, up, down):
            greet(at(p, jj))
    pl.semaphore_wait(barrier, (2 * COLS - 1) + 2 * (RING - 1) + 6)

    has_left, has_right = j > 0, j < RING - 1
    has_down, has_up = part > 0, part < 2 * COLS - 1
    x_edge = jnp.logical_or(j == 0, j == RING - 1)
    z_edge = jnp.logical_or(part == 0, part == 2 * COLS - 1)

    lower = pl.ds(4, 4)
    upper = pl.ds(0, 4)

    def halo_copies(A, send, recv):
        lo, hi = pl.ds(4, 4), pl.ds(16, 4)
        own = pl.ds(4, 16)
        below, above = pl.ds(0, 4), pl.ds(20, 4)

        def move(zs, tile, rows, zd, tiled, p, jj, group):
            remote(
                A.at[zs, tile, :, rows, :], A.at[zd, tiled, :, rows, :],
                send.at[group], recv.at[group], at(p, jj),
            ).start()

        for has_z, zs, zd, p in ((has_up, hi, below, up), (has_down, lo, above, down)):
            @pl.when(jnp.logical_and(has_z, has_left))
            def _():
                move(zs, 0, lower, zd, 1, p, left, 2)

            @pl.when(jnp.logical_and(has_z, has_right))
            def _():
                move(zs, 1, upper, zd, 0, p, right, 2)

        @pl.when(has_left)
        def _():
            move(own, 0, lower, own, 1, part, left, 0)

        @pl.when(has_right)
        def _():
            move(own, 1, upper, own, 0, part, right, 0)

        for has_z, zs, zd, p in ((has_up, hi, below, up), (has_down, lo, above, down)):
            @pl.when(has_z)
            def _():
                move(zs, 0, lower, zd, 0, p, j, 1)
                move(zs, 1, upper, zd, 1, p, j, 1)

    def await_halos(sem):
        inside = jnp.logical_not

        def await_tiles(condition, group, n):
            @pl.when(condition)
            def _():
                await_bytes(G.at[0, pl.ds(0, n // 4)], sem.at[group])

        await_tiles(inside(x_edge), 0, 32)
        await_tiles(x_edge, 0, 16)
        await_tiles(inside(z_edge), 1, 16)
        await_tiles(z_edge, 1, 8)
        await_tiles(jnp.logical_and(inside(z_edge), inside(x_edge)), 2, 16)
        await_tiles(jnp.logical_and(z_edge, inside(x_edge)), 2, 8)
        await_tiles(jnp.logical_and(inside(z_edge), x_edge), 2, 8)
        await_tiles(jnp.logical_and(z_edge, x_edge), 2, 4)

    half = j // 4
    zs = pl.ds((j % 4) * 4, 4)
    home = snake(q) == q
    stay = jnp.logical_and(c == half, home)
    for n in range(RING):
        jj = (j + n) % RING
        for a, ref in enumerate((initial, diffusion, drift)):
            src = ref.at[:, pl.ds(pl.multiple_of(jj * 8, 8), 8), :]
            dst = C.at[a, c, zs]
            if n == 0:
                @pl.when(stay)
                def _():
                    pltpu.make_async_copy(src, dst, crecv).start()

                @pl.when(jnp.logical_not(stay))
                def _():
                    remote(src, dst, csend, crecv, (snake(q) * RING + j, half)).start()
            else:
                remote(src, dst, csend, crecv, (snake(q) * RING + jj, half)).start()

    def send_forcing(first, last):
        @pl.loop(first, last)
        def _(n):
            p = (part + n) % (2 * COLS)
            remote(
                forcing.at[0, pl.ds(p * 16, 16)], F.at[2 * q + c], fsend, frecv.at[q], plane_device(p)
            ).start()

    def keep_forcing():
        pltpu.make_async_copy(forcing.at[0, pl.ds(part * 16, 16)], F.at[2 * q + c], frecv.at[q]).start()

    @pl.when(q < FIRST)
    def _():
        keep_forcing()
        send_forcing(1, 2 * COLS)

    def place(A, h, v):
        A[pl.ds(4, 16), 0, h, pl.ds(4, 4), :] = v[:, 0:4, :]
        A[pl.ds(4, 16), 1, h, pl.ds(0, 4), :] = v[:, 4:8, :]

    def clear_outside(A):
        @pl.when(part == 0)
        def _():
            A[pl.ds(0, 4)] = jnp.zeros((4, 2, 2, 8, 128), F32)

        @pl.when(part == 2 * COLS - 1)
        def _():
            A[pl.ds(20, 4)] = jnp.zeros((4, 2, 2, 8, 128), F32)

        @pl.when(j == 0)
        def _():
            A[:, 0, :, pl.ds(0, 4), :] = jnp.zeros((24, 2, 4, 128), F32)

        @pl.when(j == RING - 1)
        def _():
            A[:, 1, :, pl.ds(4, 4), :] = jnp.zeros((24, 2, 4, 128), F32)

    clear_outside(E.at[0])
    clear_outside(E.at[1])
    await_bytes(C, crecv)
    for h in range(2):
        place(D, h, C[1, h])
        place(R, h, C[2, h])
    halo_copies(D, xsend.at[0], xrecv.at[0])
    halo_copies(R, xsend.at[1], xrecv.at[1])
    for h in range(2):
        place(E.at[0], h, C[0, h])
    halo_copies(E.at[0], hsend.at[0], hrecv.at[0])

    def prepare_force(k):
        await_bytes(F.at[pl.ds(2 * k, 2)], frecv.at[k])
        clear_outside(G.at[k])
        for h in range(2):
            place(G.at[k], h, F[2 * k + h])

    def send_force(k):
        halo_copies(G.at[k], gsend.at[k], grecv.at[k])

    await_halos(xrecv.at[0])
    await_halos(xrecv.at[1])
    for z in range(0, 24, 4):
        s = pl.ds(z, 4)
        d, r = D[s], R[s]
        inv = 1.0 / (1.0 + 6.0 * d + r)
        IV[s] = inv
        DP[s] = d * inv
        EP[s] = (d + r) * inv
    for A in (IV, DP, EP):
        clear_outside(A)

    prepare_force(0)
    send_force(0)
    await_halos(hsend.at[0])

    @pl.when(q >= FIRST)
    def _():
        keep_forcing()
        send_forcing(1, 2 * COLS)

    def relax(load, load_s, z, n):
        shape = (n, 8, 128)
        row = lax.broadcasted_iota(jnp.int32, shape, 1)
        lane = lax.broadcasted_iota(jnp.int32, shape, 2)
        first_row, last_row = row == 0, row == 7
        first_lane, last_lane = lane == 0, lane == 127
        zero = jnp.zeros(shape, F32)
        wide = [[load(z - 1, n + 2, T, h) for h in range(2)] for T in range(2)]
        mid = [[wide[T][h][1:-1] for h in range(2)] for T in range(2)]
        result = [[None, None], [None, None]]
        beside = [[None, None], [None, None]]
        for h in range(2):
            a0, a1 = pltpu.roll(mid[0][h], 1, 1), pltpu.roll(mid[1][h], 1, 1)
            b0, b1 = pltpu.roll(mid[0][h], 7, 1), pltpu.roll(mid[1][h], 7, 1)
            beside[0][h] = a0 + jnp.where(last_row, b1, b0)
            beside[1][h] = jnp.where(first_row, a0, a1) + b1
        for T in range(2):
            a0, a1 = pltpu.roll(mid[T][0], 1, 2), pltpu.roll(mid[T][1], 1, 2)
            b0, b1 = pltpu.roll(mid[T][0], 127, 2), pltpu.roll(mid[T][1], 127, 2)
            across = (
                jnp.where(first_lane, zero, a0) + jnp.where(last_lane, b1, b0),
                jnp.where(first_lane, a0, a1) + jnp.where(last_lane, zero, b1),
            )
            for h in range(2):
                total = beside[T][h] + across[h] + wide[T][h][2:]
                s = pl.ds(z, n)
                result[T][h] = (
                    load_s(z, n, T, h) + DP[s, T, h] * total + EP[s, T, h] * wide[T][h][:-2]
                )
        return result

    def chunks(first, last):
        z = first
        while z < last:
            n = min(4, last - z)
            yield z, n
            z += n

    def from_ref(A):
        return lambda z, n, T, h: A[pl.ds(z, n), T, h]

    def send_state(k, piece):
        rows = 16 // PIECES
        for h in range(2):
            src = O.at[k, h, pl.ds(piece * rows, rows)]
            dst = out.at[0, pl.ds(part * 16 + piece * rows, rows)]
            mine = jnp.logical_and(k == q, c == h)

            @pl.when(mine)
            def _():
                pltpu.make_async_copy(src, dst, orecv).start()

            @pl.when(jnp.logical_not(mine))
            def _():
                remote(src, dst, osend, orecv, (k * RING + j, h)).start()

    @pl.loop(0, NT)
    def _(k):
        par = k % 2
        now, later = E.at[par], E.at[1 - par]
        force = G.at[k]
        await_halos(hrecv.at[par])
        await_halos(grecv.at[k])


        def make_source(z, n, T, h):
            s = pl.ds(z, n)
            v = (now[s, T, h] + force[s, T, h]) * IV[s, T, h]
            SP[s, T, h] = v
            return v

        for load, load_s, W, margin in (
            (from_ref(now), make_source, W1, 1),
            (from_ref(W1), from_ref(SP), W2, 2),
            (from_ref(W2), from_ref(SP), W1, 3),
        ):
            for z, n in chunks(margin, 24 - margin):
                v = relax(load, load_s, z, n)
                for T in range(2):
                    for h in range(2):
                        W[pl.ds(z, n), T, h] = v[T][h]

        for z, n in chunks(4, 20):
            v = relax(from_ref(W1), from_ref(SP), z, n)
            row = lax.broadcasted_iota(jnp.int32, (n, 8, 128), 1)
            for h in range(2):
                later[pl.ds(z, n), 0, h, pl.ds(4, 4), :] = v[0][h][:, 4:8, :]
                later[pl.ds(z, n), 1, h, pl.ds(0, 4), :] = v[1][h][:, 0:4, :]
                O[k, h, pl.ds(z - 4, n)] = jnp.where(
                    row < 4, pltpu.roll(v[0][h], 4, 1), pltpu.roll(v[1][h], 4, 1)
                )

        @pl.when(k < NT - 1)
        def _():
            halo_copies(later, hsend.at[1 - par], hrecv.at[1 - par])

        for d in range(PIECES):
            @pl.when(k >= d)
            def _():
                send_state(k - d, d)

        @pl.when(k == 0)
        def _():
            prepare_force(1)

        @pl.when(k < NT - 2)
        def _():
            prepare_force(k + 2)

        @pl.when(k < NT - 1)
        def _():
            await_halos(hsend.at[1 - par])

        @pl.when(k == 0)
        def _():
            send_force(1)

        @pl.when(k < NT - 2)
        def _():
            send_force(k + 2)

    for k in range(NT - PIECES + 1, NT):
        for piece in range(NT - k, PIECES):
            send_state(k, piece)

    @pl.when(stay)
    def _():
        await_bytes(F.at[pl.ds(0, 6), pl.ds(0, 14)], csend)

    @pl.when(jnp.logical_not(stay))
    def _():
        await_bytes(C, csend)

    await_halos(xsend.at[0])
    await_halos(xsend.at[1])

    @pl.loop(0, NT)
    def _(k):
        await_halos(gsend.at[k])

    await_bytes(F.at[pl.ds(0, 31)], fsend)
    await_bytes(F.at[pl.ds(0, 31)], osend)
    await_bytes(out, orecv)


def per_device(forcing, initial, diffusion, drift):
    wide = (24, 2, 2, 8, 128)
    vmem = lambda *shape: pltpu.VMEM(shape, F32)
    dma = pltpu.SemaphoreType.DMA
    return pl.pallas_call(
        kernel,
        out_shape=jax.ShapeDtypeStruct(forcing.shape, F32),
        in_specs=[pl.BlockSpec(memory_space=pltpu.HBM)] * 4,
        out_specs=pl.BlockSpec(memory_space=pl.ANY),
        scratch_shapes=[
            vmem(2 * NT, 16, 8, 128),
            vmem(NT, *wide),
            vmem(NT, 2, 16, 8, 128),
            vmem(2, *wide),
            vmem(3, 2, 16, 8, 128),
        ]
        + [vmem(*wide)] * 8
        + [dma, dma, dma((2, 3)), dma((2, 3)), dma, dma((NT,)), dma((NT, 3)), dma((NT, 3))]
        + [dma((2, 3)), dma((2, 3)), dma, dma],
        compiler_params=pltpu.CompilerParams(
            collective_id=0, has_side_effects=True, vmem_limit_bytes=40 * 1024 * 1024
        ),
    )(*[pltpu.with_memory_space_constraint(a, pltpu.HBM) for a in (forcing, initial, diffusion, drift)])


def solution(mesh):
    in_specs = (
        P("tm", None, None, "space"),
        P("tm", None, "space"),
        P("tm", None, "space"),
        P("tm", None, "space"),
    )
    out_specs = P("tm", None, None, "space")
    return jax.shard_map(
        per_device, mesh=mesh, in_specs=in_specs, out_specs=out_specs, check_vma=False
    )
```

```python
import jax
import jax.numpy as jnp
from jax import lax
from jax.experimental import pallas as pl
from jax.experimental.pallas import tpu as pltpu
from jax.sharding import PartitionSpec as P

NT = 16
COLS = 16
RING = 8
FIRST = 3
PIECES = 4
MESH = pl.DeviceIdType.MESH
F32 = jnp.float32


def snake(n):
    y, x = n // 4, n % 4
    return y * 4 + x + (y % 2) * (3 - 2 * x)


def remote(src, dst, send, recv, device):
    return pltpu.make_async_remote_copy(
        src_ref=src, dst_ref=dst, send_sem=send, recv_sem=recv, device_id=device, device_id_type=MESH
    )


def await_bytes(ref, sem):
    pltpu.make_async_copy(ref, ref, sem).wait()


def kernel(
    forcing, initial, diffusion, drift, out,
    G, E, D, R, DP, EP, IV, SP, W1, W2,
    csend, crecv, xsend, xrecv, fsend, frecv, gsend, grecv, hsend, hrecv, osend, orecv,
):
    t = lax.axis_index("tm")
    c = lax.axis_index("space")
    q = t // RING
    j = t % RING
    part = 2 * snake(q) + c

    def at(p, jj):
        return (snake(p // 2) * RING + jj, p % 2)

    barrier = pltpu.get_barrier_semaphore()

    def greet(device):
        pl.semaphore_signal(barrier, inc=1, device_id=device, device_id_type=MESH)

    @pl.loop(1, 2 * COLS)
    def _(n):
        greet(at((part + n) % (2 * COLS), j))

    @pl.loop(1, RING)
    def _(n):
        chip = snake(q) * RING + (j + n) % RING
        greet((chip, c))
        greet((chip, 1 - c))

    left, right = (j + RING - 1) % RING, (j + 1) % RING
    up = (part + 1) % (2 * COLS)
    down = (part + 2 * COLS - 1) % (2 * COLS)
    for jj in (left, right):
        for p in (part, up, down):
            greet(at(p, jj))

    has_left, has_right = j > 0, j < RING - 1
    has_down, has_up = part > 0, part < 2 * COLS - 1
    x_edge = jnp.logical_or(j == 0, j == RING - 1)
    z_edge = jnp.logical_or(part == 0, part == 2 * COLS - 1)
    first_rows, last_rows = pl.ds(0, 4), pl.ds(4, 4)
    own = pl.ds(4, 16)

    def clear_outside(A):
        @pl.when(part == 0)
        def _():
            A[pl.ds(0, 4)] = jnp.zeros((4, 2, 2, 8, 128), F32)

        @pl.when(part == 2 * COLS - 1)
        def _():
            A[pl.ds(20, 4)] = jnp.zeros((4, 2, 2, 8, 128), F32)

        @pl.when(j == 0)
        def _():
            A[:, 1, :, last_rows, :] = jnp.zeros((24, 2, 4, 128), F32)

        @pl.when(j == RING - 1)
        def _():
            A[:, 1, :, first_rows, :] = jnp.zeros((24, 2, 4, 128), F32)

    @pl.loop(0, NT)
    def _(k):
        clear_outside(E.at[k])
        clear_outside(G.at[k])

    pl.semaphore_wait(barrier, (2 * COLS - 1) + 2 * (RING - 1) + 6)

    def halo_copies(A, send, recv, depth):
        short = depth - 1

        def move(zs, rows, zd, tile, p, jj, group):
            remote(
                A.at[zs, 0, :, rows, :], A.at[zd, tile, :, rows, :],
                send.at[group], recv.at[group], at(p, jj),
            ).start()

        def ends(n):
            return (
                (has_up, pl.ds(20 - n, n), pl.ds(4 - n, n), up),
                (has_down, pl.ds(4, n), pl.ds(20, n), down),
            )

        for has_z, zs, zd, p in ends(short):
            @pl.when(jnp.logical_and(has_z, has_left))
            def _():
                move(zs, pl.ds(0, short), zd, 1, p, left, 2)

            @pl.when(jnp.logical_and(has_z, has_right))
            def _():
                move(zs, pl.ds(8 - short, short), zd, 1, p, right, 2)

        @pl.when(has_left)
        def _():
            move(own, pl.ds(0, depth), own, 1, part, left, 0)

        @pl.when(has_right)
        def _():
            move(own, pl.ds(8 - depth, depth), own, 1, part, right, 0)

        for has_z, zs, zd, p in ends(depth):
            @pl.when(has_z)
            def _():
                move(zs, pl.ds(0, 8), zd, 0, p, j, 1)

    def await_halos(sem, depth):
        inside = jnp.logical_not
        short = depth - 1

        def rows_of(n):
            if n % 8 == 0:
                return forcing.at[0, pl.ds(0, n // 8)]
            if n // 2 <= 24:
                return IV.at[pl.ds(0, n // 2), 0, 0, pl.ds(0, 2), :]
            return IV.at[pl.ds(0, n // 4), 0, :, pl.ds(0, 2), :]

        def await_rows(condition, group, n):
            @pl.when(condition)
            def _():
                await_bytes(rows_of(n), sem.at[group])

        await_rows(inside(x_edge), 0, 64 * depth)
        await_rows(x_edge, 0, 32 * depth)
        await_rows(inside(z_edge), 1, 32 * depth)
        await_rows(z_edge, 1, 16 * depth)
        corner = 2 * short * short
        await_rows(jnp.logical_and(inside(z_edge), inside(x_edge)), 2, 4 * corner)
        await_rows(jnp.logical_and(z_edge, inside(x_edge)), 2, 2 * corner)
        await_rows(jnp.logical_and(inside(z_edge), x_edge), 2, 2 * corner)
        await_rows(jnp.logical_and(z_edge, x_edge), 2, corner)

    def send_forcing():
        mine = G.at[q, own, 0, c]
        pltpu.make_async_copy(forcing.at[0, pl.ds(part * 16, 16)], mine, frecv.at[q]).start()

        @pl.loop(1, 2 * COLS)
        def _(n):
            p = (part + n) % (2 * COLS)
            remote(forcing.at[0, pl.ds(p * 16, 16)], mine, fsend, frecv.at[q], at(p, j)).start()

    half = j // 4
    zs = pl.ds(4 + (j % 4) * 4, 4)
    stay = jnp.logical_and(c == half, snake(q) == q)
    arriving = ((diffusion, D), (drift, R), (initial, E.at[0]))
    for a, (ref, A) in enumerate(arriving):
        for n in (4, 3, 5, 2, 6, 1, 7, 0):
            jj = (j + n) % RING
            src = ref.at[:, pl.ds(pl.multiple_of(jj * 8, 8), 8), :]
            dst = A.at[zs, 0, c]
            if n == 0:
                @pl.when(stay)
                def _():
                    pltpu.make_async_copy(src, dst, crecv.at[a]).start()

                @pl.when(jnp.logical_not(stay))
                def _():
                    remote(src, dst, csend, crecv.at[a], (snake(q) * RING + j, half)).start()
            else:
                remote(src, dst, csend, crecv.at[a], (snake(q) * RING + jj, half)).start()

    @pl.when(q < FIRST)
    def _():
        send_forcing()

    for a, (ref, A) in enumerate(arriving):
        await_bytes(forcing.at[0, pl.ds(0, 32)], crecv.at[a])
        if a < 2:
            halo_copies(A, xsend.at[a], xrecv.at[a], 3)
        else:
            halo_copies(A, hsend.at[0], hrecv.at[0], 4)

    await_halos(xrecv.at[0], 3)
    await_halos(xrecv.at[1], 3)
    for z in range(0, 24, 4):
        s = pl.ds(z, 4)
        d, r = D[s], R[s]
        inv = 1.0 / (1.0 + 6.0 * d + r)
        IV[s] = inv
        DP[s] = d * inv
        EP[s] = (d + r) * inv
    for A in (IV, DP, EP):
        clear_outside(A)

    def send_force(k):
        halo_copies(G.at[k], gsend.at[k], grecv.at[k], 3)

    def await_force(k):
        await_bytes(forcing.at[0, pl.ds(0, 32)], frecv.at[k])

    await_force(0)
    send_force(0)

    @pl.when(q >= FIRST)
    def _():
        send_forcing()

    def relax(load, load_s, z, n, tiles):
        shape = (n, 8, 128)
        row = lax.broadcasted_iota(jnp.int32, shape, 1)
        lane = lax.broadcasted_iota(jnp.int32, shape, 2)
        first_row, last_row = row == 0, row == 7
        first_lane, last_lane = lane == 0, lane == 127
        zero = jnp.zeros(shape, F32)
        wide = [[load(z - 1, n + 2, T, h) for h in range(2)] for T in range(tiles)]
        mid = [[wide[T][h][1:-1] for h in range(2)] for T in range(tiles)]
        if tiles == 1:
            mid.append([load(z, n, 1, h) for h in range(2)])
        result = [[None, None] for T in range(tiles)]
        beside = [[None, None] for T in range(tiles)]
        for h in range(2):
            a = [pltpu.roll(mid[T][h], 1, 1) for T in range(2)]
            b = [pltpu.roll(mid[T][h], 7, 1) for T in range(2)]
            for T in range(tiles):
                beside[T][h] = jnp.where(first_row, a[1 - T], a[T]) + jnp.where(last_row, b[1 - T], b[T])
        for T in range(tiles):
            a0, a1 = pltpu.roll(mid[T][0], 1, 2), pltpu.roll(mid[T][1], 1, 2)
            b0, b1 = pltpu.roll(mid[T][0], 127, 2), pltpu.roll(mid[T][1], 127, 2)
            across = (
                jnp.where(first_lane, zero, a0) + jnp.where(last_lane, b1, b0),
                jnp.where(first_lane, a0, a1) + jnp.where(last_lane, zero, b1),
            )
            for h in range(2):
                total = beside[T][h] + across[h] + wide[T][h][2:]
                s = pl.ds(z, n)
                result[T][h] = (
                    load_s(z, n, T, h) + DP[s, T, h] * total + EP[s, T, h] * wide[T][h][:-2]
                )
        return result

    def chunks(first, last):
        z = first
        while z < last:
            n = min(4, last - z)
            yield z, n
            z += n

    def from_ref(A):
        return lambda z, n, T, h: A[pl.ds(z, n), T, h]

    def send_state(k, piece):
        rows = 16 // PIECES
        for h in range(2):
            src = E.at[k + 1, pl.ds(4 + piece * rows, rows), 0, h]
            dst = out.at[0, pl.ds(part * 16 + piece * rows, rows)]
            mine = jnp.logical_and(k == q, c == h)

            @pl.when(mine)
            def _():
                pltpu.make_async_copy(src, dst, orecv).start()

            @pl.when(jnp.logical_not(mine))
            def _():
                remote(src, dst, osend, orecv, (k * RING + j, h)).start()

    @pl.loop(0, NT)
    def _(k):
        now, later = E.at[k], E.at[k + 1]
        force = G.at[k]
        await_halos(grecv.at[k], 3)
        await_halos(hrecv.at[k], 4)

        def make_source(z, n, T, h):
            s = pl.ds(z, n)
            v = (now[s, T, h] + force[s, T, h]) * IV[s, T, h]
            SP[s, T, h] = v
            return v

        for load, load_s, W, margin in (
            (from_ref(now), make_source, W1, 1),
            (from_ref(W1), from_ref(SP), W2, 2),
            (from_ref(W2), from_ref(SP), W1, 3),
        ):
            for z, n in chunks(margin, 24 - margin):
                v = relax(load, load_s, z, n, 2)
                for T in range(2):
                    for h in range(2):
                        W[pl.ds(z, n), T, h] = v[T][h]

        for z, n in chunks(4, 20):
            v = relax(from_ref(W1), from_ref(SP), z, n, 1)
            for h in range(2):
                later[pl.ds(z, n), 0, h] = v[0][h]

        @pl.when(k < NT - 1)
        def _():
            halo_copies(later, hsend.at[k + 1], hrecv.at[k + 1], 4)

        for d in range(PIECES):
            @pl.when(k >= d)
            def _():
                send_state(k - d, d)

        @pl.when(k == 0)
        def _():
            await_halos(hsend.at[0], 4)
            await_force(1)

        @pl.when(k < NT - 2)
        def _():
            await_force(k + 2)

        @pl.when(k < NT - 1)
        def _():
            await_halos(hsend.at[k + 1], 4)

        @pl.when(k == 0)
        def _():
            send_force(1)

        @pl.when(k < NT - 2)
        def _():
            send_force(k + 2)

    for k in range(NT - PIECES + 1, NT):
        for piece in range(NT - k, PIECES):
            send_state(k, piece)

    @pl.when(stay)
    def _():
        await_bytes(forcing.at[0, pl.ds(0, 84)], csend)

    @pl.when(jnp.logical_not(stay))
    def _():
        await_bytes(forcing.at[0, pl.ds(0, 96)], csend)

    await_halos(xsend.at[0], 3)
    await_halos(xsend.at[1], 3)

    @pl.loop(0, NT)
    def _(k):
        await_halos(gsend.at[k], 3)

    await_bytes(forcing.at[0, pl.ds(0, 496)], fsend)
    await_bytes(forcing.at[0, pl.ds(0, 496)], osend)
    await_bytes(out, orecv)


def per_device(forcing, initial, diffusion, drift):
    wide = (24, 2, 2, 8, 128)
    vmem = lambda *shape: pltpu.VMEM(shape, F32)
    dma = pltpu.SemaphoreType.DMA
    return pl.pallas_call(
        kernel,
        out_shape=jax.ShapeDtypeStruct(forcing.shape, F32),
        in_specs=[pl.BlockSpec(memory_space=pltpu.HBM)] * 4,
        out_specs=pl.BlockSpec(memory_space=pl.ANY),
        scratch_shapes=[vmem(NT, *wide), vmem(NT + 1, *wide)]
        + [vmem(*wide)] * 8
        + [dma, dma((3,)), dma((2, 3)), dma((2, 3)), dma, dma((NT,)), dma((NT, 3)), dma((NT, 3))]
        + [dma((NT, 3)), dma((NT, 3)), dma, dma],
        compiler_params=pltpu.CompilerParams(
            collective_id=0, has_side_effects=True, vmem_limit_bytes=40 * 1024 * 1024
        ),
    )(*[pltpu.with_memory_space_constraint(a, pltpu.HBM) for a in (forcing, initial, diffusion, drift)])


def solution(mesh):
    in_specs = (
        P("tm", None, None, "space"),
        P("tm", None, "space"),
        P("tm", None, "space"),
        P("tm", None, "space"),
    )
    out_specs = P("tm", None, None, "space")
    return jax.shard_map(
        per_device, mesh=mesh, in_specs=in_specs, out_specs=out_specs, check_vma=False
    )
```

```python
import jax
import jax.numpy as jnp
from jax import lax
from jax.experimental import pallas as pl
from jax.experimental.pallas import tpu as pltpu
from jax.sharding import PartitionSpec as P

NT = 16
COLS = 16
RING = 8
PIECES = 4
MESH = pl.DeviceIdType.MESH
F32 = jnp.float32


def snake(n):
    y, x = n // 4, n % 4
    return y * 4 + x + (y % 2) * (3 - 2 * x)


def remote(src, dst, send, recv, device):
    return pltpu.make_async_remote_copy(
        src_ref=src, dst_ref=dst, send_sem=send, recv_sem=recv, device_id=device, device_id_type=MESH
    )


def await_bytes(ref, sem):
    pltpu.make_async_copy(ref, ref, sem).wait()


def kernel(
    forcing, initial, diffusion, drift, out,
    G, E, D, R, DP, EP, IV, SP, W1, W2,
    csend, crecv, xsend, xrecv, fsend, frecv, gsend, grecv, hsend, hrecv, osend, orecv,
):
    t = lax.axis_index("tm")
    c = lax.axis_index("space")
    q = t // RING
    j = t % RING
    part = 2 * snake(q) + c

    def at(p, jj):
        return (snake(p // 2) * RING + jj, p % 2)

    barrier = pltpu.get_barrier_semaphore()

    def greet(device):
        pl.semaphore_signal(barrier, inc=1, device_id=device, device_id_type=MESH)

    @pl.loop(1, 2 * COLS)
    def _(n):
        greet(at((part + n) % (2 * COLS), j))

    @pl.loop(1, RING)
    def _(n):
        chip = snake(q) * RING + (j + n) % RING
        greet((chip, c))
        greet((chip, 1 - c))

    left, right = (j + RING - 1) % RING, (j + 1) % RING
    up = (part + 1) % (2 * COLS)
    down = (part + 2 * COLS - 1) % (2 * COLS)
    for jj in (left, right):
        for p in (part, up, down):
            greet(at(p, jj))

    has_left, has_right = j > 0, j < RING - 1
    has_down, has_up = part > 0, part < 2 * COLS - 1
    x_edge = jnp.logical_or(j == 0, j == RING - 1)
    z_edge = jnp.logical_or(part == 0, part == 2 * COLS - 1)
    first_rows, last_rows = pl.ds(0, 4), pl.ds(4, 4)
    own = pl.ds(4, 16)

    def clear_outside(A):
        @pl.when(part == 0)
        def _():
            A[pl.ds(0, 4)] = jnp.zeros((4, 2, 2, 8, 128), F32)

        @pl.when(part == 2 * COLS - 1)
        def _():
            A[pl.ds(20, 4)] = jnp.zeros((4, 2, 2, 8, 128), F32)

        @pl.when(j == 0)
        def _():
            A[:, 1, :, last_rows, :] = jnp.zeros((24, 2, 4, 128), F32)

        @pl.when(j == RING - 1)
        def _():
            A[:, 1, :, first_rows, :] = jnp.zeros((24, 2, 4, 128), F32)

    @pl.loop(0, NT)
    def _(k):
        clear_outside(E.at[k])
        clear_outside(G.at[k])

    pl.semaphore_wait(barrier, (2 * COLS - 1) + 2 * (RING - 1) + 6)

    def halo_copies(A, send, recv, depth):
        short = depth - 1

        def move(zs, rows, zd, tile, p, jj, group):
            remote(
                A.at[zs, 0, :, rows, :], A.at[zd, tile, :, rows, :],
                send.at[group], recv.at[group], at(p, jj),
            ).start()

        def ends(n):
            return (
                (has_up, pl.ds(20 - n, n), pl.ds(4 - n, n), up),
                (has_down, pl.ds(4, n), pl.ds(20, n), down),
            )

        for has_z, zs, zd, p in ends(short):
            @pl.when(jnp.logical_and(has_z, has_left))
            def _():
                move(zs, pl.ds(0, short), zd, 1, p, left, 2)

            @pl.when(jnp.logical_and(has_z, has_right))
            def _():
                move(zs, pl.ds(8 - short, short), zd, 1, p, right, 2)

        @pl.when(has_left)
        def _():
            move(own, pl.ds(0, depth), own, 1, part, left, 0)

        @pl.when(has_right)
        def _():
            move(own, pl.ds(8 - depth, depth), own, 1, part, right, 0)

        for has_z, zs, zd, p in ends(depth):
            @pl.when(has_z)
            def _():
                move(zs, pl.ds(0, 8), zd, 0, p, j, 1)

    def await_halos(sem, depth):
        inside = jnp.logical_not
        short = depth - 1

        def rows_of(n):
            if n % 8 == 0:
                return forcing.at[0, pl.ds(0, n // 8)]
            if n // 2 <= 24:
                return IV.at[pl.ds(0, n // 2), 0, 0, pl.ds(0, 2), :]
            return IV.at[pl.ds(0, n // 4), 0, :, pl.ds(0, 2), :]

        def await_rows(condition, group, n):
            @pl.when(condition)
            def _():
                await_bytes(rows_of(n), sem.at[group])

        await_rows(inside(x_edge), 0, 64 * depth)
        await_rows(x_edge, 0, 32 * depth)
        await_rows(inside(z_edge), 1, 32 * depth)
        await_rows(z_edge, 1, 16 * depth)
        corner = 2 * short * short
        await_rows(jnp.logical_and(inside(z_edge), inside(x_edge)), 2, 4 * corner)
        await_rows(jnp.logical_and(z_edge, inside(x_edge)), 2, 2 * corner)
        await_rows(jnp.logical_and(inside(z_edge), x_edge), 2, 2 * corner)
        await_rows(jnp.logical_and(z_edge, x_edge), 2, corner)

    def send_forcing():
        mine = G.at[q, own, 0, c]
        pltpu.make_async_copy(forcing.at[0, pl.ds(part * 16, 16)], mine, frecv.at[q]).start()

        @pl.loop(1, 2 * COLS)
        def _(n):
            p = (part + 13 * n) % (2 * COLS)
            remote(forcing.at[0, pl.ds(p * 16, 16)], mine, fsend, frecv.at[q], at(p, j)).start()

    half = j // 4
    zs = pl.ds(4 + (j % 4) * 4, 4)
    stay = jnp.logical_and(c == half, snake(q) == q)
    arriving = ((diffusion, D), (drift, R), (initial, E.at[0]))
    for a, (ref, A) in enumerate(arriving):
        for n in (4, 3, 5, 2, 6, 1, 7, 0):
            jj = (j + n) % RING
            src = ref.at[:, pl.ds(pl.multiple_of(jj * 8, 8), 8), :]
            dst = A.at[zs, 0, c]
            if n == 0:
                @pl.when(stay)
                def _():
                    pltpu.make_async_copy(src, dst, crecv.at[a]).start()

                @pl.when(jnp.logical_not(stay))
                def _():
                    remote(src, dst, csend, crecv.at[a], (snake(q) * RING + j, half)).start()
            else:
                remote(src, dst, csend, crecv.at[a], (snake(q) * RING + jj, half)).start()

    send_forcing()

    for a, (ref, A) in enumerate(arriving):
        await_bytes(forcing.at[0, pl.ds(0, 32)], crecv.at[a])
        if a < 2:
            halo_copies(A, xsend.at[a], xrecv.at[a], 3)
        else:
            halo_copies(A, hsend.at[0], hrecv.at[0], 4)

    await_halos(xrecv.at[0], 3)
    await_halos(xrecv.at[1], 3)
    for z in range(0, 24, 4):
        s = pl.ds(z, 4)
        d, r = D[s], R[s]
        inv = 1.0 / (1.0 + 6.0 * d + r)
        IV[s] = inv
        DP[s] = d * inv
        EP[s] = (d + r) * inv
    for A in (IV, DP, EP):
        clear_outside(A)

    def send_force(k):
        halo_copies(G.at[k], gsend.at[k], grecv.at[k], 3)

    def await_force(k):
        await_bytes(forcing.at[0, pl.ds(0, 32)], frecv.at[k])

    await_force(0)
    send_force(0)

    def relax(load, load_s, z, n, tiles):
        shape = (n, 8, 128)
        row = lax.broadcasted_iota(jnp.int32, shape, 1)
        lane = lax.broadcasted_iota(jnp.int32, shape, 2)
        first_row, last_row = row == 0, row == 7
        first_lane, last_lane = lane == 0, lane == 127
        zero = jnp.zeros(shape, F32)
        wide = [[load(z - 1, n + 2, T, h) for h in range(2)] for T in range(tiles)]
        mid = [[wide[T][h][1:-1] for h in range(2)] for T in range(tiles)]
        if tiles == 1:
            mid.append([load(z, n, 1, h) for h in range(2)])
        result = [[None, None] for T in range(tiles)]
        beside = [[None, None] for T in range(tiles)]
        for h in range(2):
            a = [pltpu.roll(mid[T][h], 1, 1) for T in range(2)]
            b = [pltpu.roll(mid[T][h], 7, 1) for T in range(2)]
            for T in range(tiles):
                beside[T][h] = jnp.where(first_row, a[1 - T], a[T]) + jnp.where(last_row, b[1 - T], b[T])
        for T in range(tiles):
            a0, a1 = pltpu.roll(mid[T][0], 1, 2), pltpu.roll(mid[T][1], 1, 2)
            b0, b1 = pltpu.roll(mid[T][0], 127, 2), pltpu.roll(mid[T][1], 127, 2)
            across = (
                jnp.where(first_lane, zero, a0) + jnp.where(last_lane, b1, b0),
                jnp.where(first_lane, a0, a1) + jnp.where(last_lane, zero, b1),
            )
            for h in range(2):
                total = beside[T][h] + across[h] + wide[T][h][2:]
                s = pl.ds(z, n)
                result[T][h] = (
                    load_s(z, n, T, h) + DP[s, T, h] * total + EP[s, T, h] * wide[T][h][:-2]
                )
        return result

    def chunks(first, last):
        z = first
        while z < last:
            n = min(4, last - z)
            yield z, n
            z += n

    def from_ref(A):
        return lambda z, n, T, h: A[pl.ds(z, n), T, h]

    def send_state(k, piece):
        rows = 16 // PIECES
        for h in range(2):
            src = E.at[k + 1, pl.ds(4 + piece * rows, rows), 0, h]
            dst = out.at[0, pl.ds(part * 16 + piece * rows, rows)]
            mine = jnp.logical_and(k == q, c == h)

            @pl.when(mine)
            def _():
                pltpu.make_async_copy(src, dst, orecv).start()

            @pl.when(jnp.logical_not(mine))
            def _():
                remote(src, dst, osend, orecv, (k * RING + j, h)).start()

    @pl.loop(0, NT)
    def _(k):
        now, later = E.at[k], E.at[k + 1]
        force = G.at[k]
        await_halos(grecv.at[k], 3)
        await_halos(hrecv.at[k], 4)

        def make_source(z, n, T, h):
            s = pl.ds(z, n)
            v = (now[s, T, h] + force[s, T, h]) * IV[s, T, h]
            SP[s, T, h] = v
            return v

        for load, load_s, W, margin in (
            (from_ref(now), make_source, W1, 1),
            (from_ref(W1), from_ref(SP), W2, 2),
            (from_ref(W2), from_ref(SP), W1, 3),
        ):
            for z, n in chunks(margin, 24 - margin):
                v = relax(load, load_s, z, n, 2)
                for T in range(2):
                    for h in range(2):
                        W[pl.ds(z, n), T, h] = v[T][h]

        for z, n in chunks(4, 20):
            v = relax(from_ref(W1), from_ref(SP), z, n, 1)
            for h in range(2):
                later[pl.ds(z, n), 0, h] = v[0][h]

        @pl.when(k < NT - 1)
        def _():
            halo_copies(later, hsend.at[k + 1], hrecv.at[k + 1], 4)

        for d in range(PIECES):
            @pl.when(k >= d)
            def _():
                send_state(k - d, d)

        @pl.when(k == 0)
        def _():
            await_halos(hsend.at[0], 4)
            await_force(1)

        @pl.when(k < NT - 2)
        def _():
            await_force(k + 2)

        @pl.when(k < NT - 1)
        def _():
            await_halos(hsend.at[k + 1], 4)

        @pl.when(k == 0)
        def _():
            send_force(1)

        @pl.when(k < NT - 2)
        def _():
            send_force(k + 2)

    for k in range(NT - PIECES + 1, NT):
        for piece in range(NT - k, PIECES):
            send_state(k, piece)

    @pl.when(stay)
    def _():
        await_bytes(forcing.at[0, pl.ds(0, 84)], csend)

    @pl.when(jnp.logical_not(stay))
    def _():
        await_bytes(forcing.at[0, pl.ds(0, 96)], csend)

    await_halos(xsend.at[0], 3)
    await_halos(xsend.at[1], 3)

    @pl.loop(0, NT)
    def _(k):
        await_halos(gsend.at[k], 3)

    await_bytes(forcing.at[0, pl.ds(0, 496)], fsend)
    await_bytes(forcing.at[0, pl.ds(0, 496)], osend)
    await_bytes(out, orecv)


def per_device(forcing, initial, diffusion, drift):
    wide = (24, 2, 2, 8, 128)
    vmem = lambda *shape: pltpu.VMEM(shape, F32)
    dma = pltpu.SemaphoreType.DMA
    return pl.pallas_call(
        kernel,
        out_shape=jax.ShapeDtypeStruct(forcing.shape, F32),
        in_specs=[pl.BlockSpec(memory_space=pltpu.HBM)] * 4,
        out_specs=pl.BlockSpec(memory_space=pl.ANY),
        scratch_shapes=[vmem(NT, *wide), vmem(NT + 1, *wide)]
        + [vmem(*wide)] * 8
        + [dma, dma((3,)), dma((2, 3)), dma((2, 3)), dma, dma((NT,)), dma((NT, 3)), dma((NT, 3))]
        + [dma((NT, 3)), dma((NT, 3)), dma, dma],
        compiler_params=pltpu.CompilerParams(
            collective_id=0, has_side_effects=True, vmem_limit_bytes=40 * 1024 * 1024
        ),
    )(*[pltpu.with_memory_space_constraint(a, pltpu.HBM) for a in (forcing, initial, diffusion, drift)])


def solution(mesh):
    in_specs = (
        P("tm", None, None, "space"),
        P("tm", None, "space"),
        P("tm", None, "space"),
        P("tm", None, "space"),
    )
    out_specs = P("tm", None, None, "space")
    return jax.shard_map(
        per_device, mesh=mesh, in_specs=in_specs, out_specs=out_specs, check_vma=False
    )
```

```python
import jax
import jax.numpy as jnp
from jax import lax
from jax.experimental import pallas as pl
from jax.experimental.pallas import tpu as pltpu
from jax.sharding import PartitionSpec as P

NT = 16
COLS = 16
RING = 8
PIECES = 4
MESH = pl.DeviceIdType.MESH
F32 = jnp.float32


def snake(n):
    y, x = n // 4, n % 4
    return y * 4 + x + (y % 2) * (3 - 2 * x)


def remote(src, dst, send, recv, device):
    return pltpu.make_async_remote_copy(
        src_ref=src, dst_ref=dst, send_sem=send, recv_sem=recv, device_id=device, device_id_type=MESH
    )


def await_bytes(ref, sem):
    pltpu.make_async_copy(ref, ref, sem).wait()


def kernel(
    forcing, initial, diffusion, drift, out,
    G, E, D, R, DP, EP, IV, SP, W1, W2,
    csend, crecv, xsend, xrecv, fsend, frecv, gsend, grecv, hsend, hrecv, osend, orecv,
):
    t = lax.axis_index("tm")
    c = lax.axis_index("space")
    q = t // RING
    j = t % RING
    part = 2 * snake(q) + c

    def at(p, jj):
        return (snake(p // 2) * RING + jj, p % 2)

    barrier = pltpu.get_barrier_semaphore()

    def greet(device):
        pl.semaphore_signal(barrier, inc=1, device_id=device, device_id_type=MESH)

    @pl.loop(1, 2 * COLS)
    def _(n):
        greet(at((part + n) % (2 * COLS), j))

    @pl.loop(1, RING)
    def _(n):
        chip = snake(q) * RING + (j + n) % RING
        greet((chip, c))
        greet((chip, 1 - c))

    left, right = (j + RING - 1) % RING, (j + 1) % RING
    up = (part + 1) % (2 * COLS)
    down = (part + 2 * COLS - 1) % (2 * COLS)
    for jj in (left, right):
        for p in (part, up, down):
            greet(at(p, jj))

    has_left, has_right = j > 0, j < RING - 1
    has_down, has_up = part > 0, part < 2 * COLS - 1
    x_edge = jnp.logical_or(j == 0, j == RING - 1)
    z_edge = jnp.logical_or(part == 0, part == 2 * COLS - 1)
    first_rows, last_rows = pl.ds(0, 4), pl.ds(4, 4)
    own = pl.ds(4, 16)

    def clear_outside(A):
        @pl.when(part == 0)
        def _():
            A[pl.ds(0, 4)] = jnp.zeros((4, 2, 2, 8, 128), F32)

        @pl.when(part == 2 * COLS - 1)
        def _():
            A[pl.ds(20, 4)] = jnp.zeros((4, 2, 2, 8, 128), F32)

        @pl.when(j == 0)
        def _():
            A[:, 1, :, last_rows, :] = jnp.zeros((24, 2, 4, 128), F32)

        @pl.when(j == RING - 1)
        def _():
            A[:, 1, :, first_rows, :] = jnp.zeros((24, 2, 4, 128), F32)

    @pl.loop(0, NT)
    def _(k):
        clear_outside(E.at[k])
        clear_outside(G.at[k])

    pl.semaphore_wait(barrier, (2 * COLS - 1) + 2 * (RING - 1) + 6)

    def halo_copies(A, send, recv, depth, stage=None):
        short = depth - 1

        def move(zs, rows, zd, tile, p, jj, group):
            remote(
                A.at[zs, 0, :, rows, :], A.at[zd, tile, :, rows, :],
                send.at[group], recv.at[group], at(p, jj),
            ).start()

        def ends(n):
            return (
                (has_up, pl.ds(20 - n, n), pl.ds(4 - n, n), up),
                (has_down, pl.ds(4, n), pl.ds(20, n), down),
            )

        for has_z, zs, zd, p in () if stage == 1 else ends(short):
            @pl.when(jnp.logical_and(has_z, has_left))
            def _():
                move(zs, pl.ds(0, short), zd, 1, p, left, 2)

            @pl.when(jnp.logical_and(has_z, has_right))
            def _():
                move(zs, pl.ds(8 - short, short), zd, 1, p, right, 2)

        if stage == 0:
            return

        @pl.when(has_left)
        def _():
            move(own, pl.ds(0, depth), own, 1, part, left, 0)

        @pl.when(has_right)
        def _():
            move(own, pl.ds(8 - depth, depth), own, 1, part, right, 0)

        for has_z, zs, zd, p in ends(depth):
            @pl.when(has_z)
            def _():
                move(zs, pl.ds(0, 8), zd, 0, p, j, 1)

    def await_halos(sem, depth):
        inside = jnp.logical_not
        short = depth - 1

        def rows_of(n):
            if n % 8 == 0:
                return forcing.at[0, pl.ds(0, n // 8)]
            if n // 2 <= 24:
                return IV.at[pl.ds(0, n // 2), 0, 0, pl.ds(0, 2), :]
            return IV.at[pl.ds(0, n // 4), 0, :, pl.ds(0, 2), :]

        def await_rows(condition, group, n):
            @pl.when(condition)
            def _():
                await_bytes(rows_of(n), sem.at[group])

        await_rows(inside(x_edge), 0, 64 * depth)
        await_rows(x_edge, 0, 32 * depth)
        await_rows(inside(z_edge), 1, 32 * depth)
        await_rows(z_edge, 1, 16 * depth)
        corner = 2 * short * short
        await_rows(jnp.logical_and(inside(z_edge), inside(x_edge)), 2, 4 * corner)
        await_rows(jnp.logical_and(z_edge, inside(x_edge)), 2, 2 * corner)
        await_rows(jnp.logical_and(inside(z_edge), x_edge), 2, 2 * corner)
        await_rows(jnp.logical_and(z_edge, x_edge), 2, corner)

    def send_forcing(first, last):
        mine = G.at[q, own, 0, c]
        if first == 1:
            pltpu.make_async_copy(forcing.at[0, pl.ds(part * 16, 16)], mine, frecv.at[q]).start()

        @pl.loop(first, last)
        def _(n):
            p = (part + 13 * n) % (2 * COLS)
            remote(forcing.at[0, pl.ds(p * 16, 16)], mine, fsend, frecv.at[q], at(p, j)).start()

    half = j // 4
    zs = pl.ds(4 + (j % 4) * 4, 4)
    stay = jnp.logical_and(c == half, snake(q) == q)
    arriving = ((diffusion, D), (drift, R), (initial, E.at[0]))
    for a, (ref, A) in enumerate(arriving):
        for n in (4, 3, 5, 2, 6, 1, 7, 0):
            jj = (j + n) % RING
            src = ref.at[:, pl.ds(pl.multiple_of(jj * 8, 8), 8), :]
            dst = A.at[zs, 0, c]
            if n == 0:
                @pl.when(stay)
                def _():
                    pltpu.make_async_copy(src, dst, crecv.at[a]).start()

                @pl.when(jnp.logical_not(stay))
                def _():
                    remote(src, dst, csend, crecv.at[a], (snake(q) * RING + j, half)).start()
            else:
                remote(src, dst, csend, crecv.at[a], (snake(q) * RING + jj, half)).start()

    send_forcing(1, 16)

    @pl.when(q < 4)
    def _():
        send_forcing(16, 2 * COLS)

    for a, (ref, A) in enumerate(arriving):
        await_bytes(forcing.at[0, pl.ds(0, 32)], crecv.at[a])
        if a < 2:
            halo_copies(A, xsend.at[a], xrecv.at[a], 3)
        else:
            halo_copies(A, hsend.at[0], hrecv.at[0], 4)

    @pl.when(q >= 4)
    def _():
        send_forcing(16, 2 * COLS)

    await_halos(xrecv.at[0], 3)
    await_halos(xrecv.at[1], 3)
    for z in range(0, 24, 4):
        s = pl.ds(z, 4)
        d, r = D[s], R[s]
        inv = 1.0 / (1.0 + 6.0 * d + r)
        IV[s] = inv
        DP[s] = d * inv
        EP[s] = (d + r) * inv
    for A in (IV, DP, EP):
        clear_outside(A)

    def send_force(k):
        halo_copies(G.at[k], gsend.at[k], grecv.at[k], 3)

    def await_force(k):
        await_bytes(forcing.at[0, pl.ds(0, 32)], frecv.at[k])

    await_force(0)
    send_force(0)

    def relax(load, load_s, z, n, tiles):
        shape = (n, 8, 128)
        row = lax.broadcasted_iota(jnp.int32, shape, 1)
        lane = lax.broadcasted_iota(jnp.int32, shape, 2)
        first_row, last_row = row == 0, row == 7
        first_lane, last_lane = lane == 0, lane == 127
        zero = jnp.zeros(shape, F32)
        wide = [[load(z - 1, n + 2, T, h) for h in range(2)] for T in range(tiles)]
        mid = [[wide[T][h][1:-1] for h in range(2)] for T in range(tiles)]
        if tiles == 1:
            mid.append([load(z, n, 1, h) for h in range(2)])
        result = [[None, None] for T in range(tiles)]
        beside = [[None, None] for T in range(tiles)]
        for h in range(2):
            a = [pltpu.roll(mid[T][h], 1, 1) for T in range(2)]
            b = [pltpu.roll(mid[T][h], 7, 1) for T in range(2)]
            for T in range(tiles):
                beside[T][h] = jnp.where(first_row, a[1 - T], a[T]) + jnp.where(last_row, b[1 - T], b[T])
        for T in range(tiles):
            a0, a1 = pltpu.roll(mid[T][0], 1, 2), pltpu.roll(mid[T][1], 1, 2)
            b0, b1 = pltpu.roll(mid[T][0], 127, 2), pltpu.roll(mid[T][1], 127, 2)
            across = (
                jnp.where(first_lane, zero, a0) + jnp.where(last_lane, b1, b0),
                jnp.where(first_lane, a0, a1) + jnp.where(last_lane, zero, b1),
            )
            for h in range(2):
                total = beside[T][h] + across[h] + wide[T][h][2:]
                s = pl.ds(z, n)
                result[T][h] = (
                    load_s(z, n, T, h) + DP[s, T, h] * total + EP[s, T, h] * wide[T][h][:-2]
                )
        return result

    def chunks(first, last):
        z = first
        while z < last:
            n = min(4, last - z)
            yield z, n
            z += n

    def from_ref(A):
        return lambda z, n, T, h: A[pl.ds(z, n), T, h]

    def send_state(k, piece):
        rows = 16 // PIECES
        for h in range(2):
            src = E.at[k + 1, pl.ds(4 + piece * rows, rows), 0, h]
            dst = out.at[0, pl.ds(part * 16 + piece * rows, rows)]
            mine = jnp.logical_and(k == q, c == h)

            @pl.when(mine)
            def _():
                pltpu.make_async_copy(src, dst, orecv).start()

            @pl.when(jnp.logical_not(mine))
            def _():
                remote(src, dst, osend, orecv, (k * RING + j, h)).start()

    @pl.loop(0, NT)
    def _(k):
        now, later = E.at[k], E.at[k + 1]
        force = G.at[k]
        await_halos(grecv.at[k], 3)
        await_halos(hrecv.at[k], 4)

        def make_source(z, n, T, h):
            s = pl.ds(z, n)
            v = (now[s, T, h] + force[s, T, h]) * IV[s, T, h]
            SP[s, T, h] = v
            return v

        for load, load_s, W, margin in (
            (from_ref(now), make_source, W1, 1),
            (from_ref(W1), from_ref(SP), W2, 2),
            (from_ref(W2), from_ref(SP), W1, 3),
        ):
            for z, n in chunks(margin, 24 - margin):
                v = relax(load, load_s, z, n, 2)
                for T in range(2):
                    for h in range(2):
                        W[pl.ds(z, n), T, h] = v[T][h]

        for z, n in ((4, 4), (16, 4), (8, 4), (12, 4)):
            if z == 8:
                @pl.when(k < NT - 1)
                def _():
                    halo_copies(later, hsend.at[k + 1], hrecv.at[k + 1], 4, 0)

            v = relax(from_ref(W1), from_ref(SP), z, n, 1)
            for h in range(2):
                later[pl.ds(z, n), 0, h] = v[0][h]

        @pl.when(k < NT - 1)
        def _():
            halo_copies(later, hsend.at[k + 1], hrecv.at[k + 1], 4, 1)

        for d in range(PIECES):
            @pl.when(k >= d)
            def _():
                send_state(k - d, d)

        @pl.when(k == 0)
        def _():
            await_halos(hsend.at[0], 4)
            await_force(1)

        @pl.when(k < NT - 2)
        def _():
            await_force(k + 2)

        @pl.when(k < NT - 1)
        def _():
            await_halos(hsend.at[k + 1], 4)

        @pl.when(k == 0)
        def _():
            send_force(1)

        @pl.when(k < NT - 2)
        def _():
            send_force(k + 2)

    for k in range(NT - PIECES + 1, NT):
        for piece in range(NT - k, PIECES):
            send_state(k, piece)

    @pl.when(stay)
    def _():
        await_bytes(forcing.at[0, pl.ds(0, 84)], csend)

    @pl.when(jnp.logical_not(stay))
    def _():
        await_bytes(forcing.at[0, pl.ds(0, 96)], csend)

    await_halos(xsend.at[0], 3)
    await_halos(xsend.at[1], 3)

    @pl.loop(0, NT)
    def _(k):
        await_halos(gsend.at[k], 3)

    await_bytes(forcing.at[0, pl.ds(0, 496)], fsend)
    await_bytes(forcing.at[0, pl.ds(0, 496)], osend)
    await_bytes(out, orecv)


def per_device(forcing, initial, diffusion, drift):
    wide = (24, 2, 2, 8, 128)
    vmem = lambda *shape: pltpu.VMEM(shape, F32)
    dma = pltpu.SemaphoreType.DMA
    return pl.pallas_call(
        kernel,
        out_shape=jax.ShapeDtypeStruct(forcing.shape, F32),
        in_specs=[pl.BlockSpec(memory_space=pltpu.HBM)] * 4,
        out_specs=pl.BlockSpec(memory_space=pl.ANY),
        scratch_shapes=[vmem(NT, *wide), vmem(NT + 1, *wide)]
        + [vmem(*wide)] * 8
        + [dma, dma((3,)), dma((2, 3)), dma((2, 3)), dma, dma((NT,)), dma((NT, 3)), dma((NT, 3))]
        + [dma((NT, 3)), dma((NT, 3)), dma, dma],
        compiler_params=pltpu.CompilerParams(
            collective_id=0, has_side_effects=True, vmem_limit_bytes=40 * 1024 * 1024
        ),
    )(*[pltpu.with_memory_space_constraint(a, pltpu.HBM) for a in (forcing, initial, diffusion, drift)])


def solution(mesh):
    in_specs = (
        P("tm", None, None, "space"),
        P("tm", None, "space"),
        P("tm", None, "space"),
        P("tm", None, "space"),
    )
    out_specs = P("tm", None, None, "space")
    return jax.shard_map(
        per_device, mesh=mesh, in_specs=in_specs, out_specs=out_specs, check_vma=False
    )
```

```python
import jax
import jax.numpy as jnp
from jax import lax
from jax.experimental import pallas as pl
from jax.experimental.pallas import tpu as pltpu
from jax.sharding import PartitionSpec as P

NT = 16
COLS = 16
RING = 8
PIECES = 4
MESH = pl.DeviceIdType.MESH
F32 = jnp.float32


def snake(n):
    y, x = n // 4, n % 4
    return y * 4 + x + (y % 2) * (3 - 2 * x)


def remote(src, dst, send, recv, device):
    return pltpu.make_async_remote_copy(
        src_ref=src, dst_ref=dst, send_sem=send, recv_sem=recv, device_id=device, device_id_type=MESH
    )


def await_bytes(ref, sem):
    pltpu.make_async_copy(ref, ref, sem).wait()


def kernel(
    forcing, initial, diffusion, drift, out,
    G, E, D, R, DP, EP, IV, SP, W1, W2,
    csend, crecv, xsend, xrecv, fsend, frecv, gsend, grecv, hsend, hrecv, osend, orecv,
):
    t = lax.axis_index("tm")
    c = lax.axis_index("space")
    q = t // RING
    j = t % RING
    part = 2 * snake(q) + c

    def at(p, jj):
        return (snake(p // 2) * RING + jj, p % 2)

    barrier = pltpu.get_barrier_semaphore()

    def greet(device):
        pl.semaphore_signal(barrier, inc=1, device_id=device, device_id_type=MESH)

    @pl.loop(1, 2 * COLS)
    def _(n):
        greet(at((part + n) % (2 * COLS), j))

    @pl.loop(1, RING)
    def _(n):
        chip = snake(q) * RING + (j + n) % RING
        greet((chip, c))
        greet((chip, 1 - c))

    left, right = (j + RING - 1) % RING, (j + 1) % RING
    up = (part + 1) % (2 * COLS)
    down = (part + 2 * COLS - 1) % (2 * COLS)
    for jj in (left, right):
        for p in (part, up, down):
            greet(at(p, jj))

    has_left, has_right = j > 0, j < RING - 1
    has_down, has_up = part > 0, part < 2 * COLS - 1
    x_edge = jnp.logical_or(j == 0, j == RING - 1)
    z_edge = jnp.logical_or(part == 0, part == 2 * COLS - 1)
    first_rows, last_rows = pl.ds(0, 4), pl.ds(4, 4)
    own = pl.ds(4, 16)

    def clear_outside(A):
        @pl.when(part == 0)
        def _():
            A[pl.ds(0, 4)] = jnp.zeros((4, 2, 2, 8, 128), F32)

        @pl.when(part == 2 * COLS - 1)
        def _():
            A[pl.ds(20, 4)] = jnp.zeros((4, 2, 2, 8, 128), F32)

        @pl.when(j == 0)
        def _():
            A[:, 1, :, last_rows, :] = jnp.zeros((24, 2, 4, 128), F32)

        @pl.when(j == RING - 1)
        def _():
            A[:, 1, :, first_rows, :] = jnp.zeros((24, 2, 4, 128), F32)

    @pl.loop(0, NT)
    def _(k):
        clear_outside(E.at[k])
        clear_outside(G.at[k])

    pl.semaphore_wait(barrier, (2 * COLS - 1) + 2 * (RING - 1) + 6)

    def halo_copies(A, send, recv, depth, stage=None):
        short = depth - 1

        def move(zs, rows, zd, tile, p, jj, group):
            remote(
                A.at[zs, 0, :, rows, :], A.at[zd, tile, :, rows, :],
                send.at[group], recv.at[group], at(p, jj),
            ).start()

        def ends(n):
            return (
                (has_up, pl.ds(20 - n, n), pl.ds(4 - n, n), up),
                (has_down, pl.ds(4, n), pl.ds(20, n), down),
            )

        for has_z, zs, zd, p in () if stage == 1 else ends(short):
            @pl.when(jnp.logical_and(has_z, has_left))
            def _():
                move(zs, pl.ds(0, short), zd, 1, p, left, 2)

            @pl.when(jnp.logical_and(has_z, has_right))
            def _():
                move(zs, pl.ds(8 - short, short), zd, 1, p, right, 2)

        for has_z, zs, zd, p in () if stage == 1 else ends(depth):
            @pl.when(has_z)
            def _():
                move(zs, pl.ds(0, 8), zd, 0, p, j, 1)

        if stage == 0:
            return

        @pl.when(has_left)
        def _():
            move(own, pl.ds(0, depth), own, 1, part, left, 0)

        @pl.when(has_right)
        def _():
            move(own, pl.ds(8 - depth, depth), own, 1, part, right, 0)

    def await_halos(sem, depth):
        inside = jnp.logical_not
        short = depth - 1

        def rows_of(n):
            if n % 8 == 0:
                return forcing.at[0, pl.ds(0, n // 8)]
            if n // 2 <= 24:
                return IV.at[pl.ds(0, n // 2), 0, 0, pl.ds(0, 2), :]
            return IV.at[pl.ds(0, n // 4), 0, :, pl.ds(0, 2), :]

        def await_rows(condition, group, n):
            @pl.when(condition)
            def _():
                await_bytes(rows_of(n), sem.at[group])

        await_rows(inside(x_edge), 0, 64 * depth)
        await_rows(x_edge, 0, 32 * depth)
        await_rows(inside(z_edge), 1, 32 * depth)
        await_rows(z_edge, 1, 16 * depth)
        corner = 2 * short * short
        await_rows(jnp.logical_and(inside(z_edge), inside(x_edge)), 2, 4 * corner)
        await_rows(jnp.logical_and(z_edge, inside(x_edge)), 2, 2 * corner)
        await_rows(jnp.logical_and(inside(z_edge), x_edge), 2, 2 * corner)
        await_rows(jnp.logical_and(z_edge, x_edge), 2, corner)

    def send_forcing(first, last):
        mine = G.at[q, own, 0, c]
        if first == 1:
            pltpu.make_async_copy(forcing.at[0, pl.ds(part * 16, 16)], mine, frecv.at[q]).start()

        @pl.loop(first, last)
        def _(n):
            p = (part + 13 * n) % (2 * COLS)
            remote(forcing.at[0, pl.ds(p * 16, 16)], mine, fsend, frecv.at[q], at(p, j)).start()

    half = j // 4
    zs = pl.ds(4 + (j % 4) * 4, 4)
    stay = jnp.logical_and(c == half, snake(q) == q)
    arriving = ((diffusion, D), (drift, R), (initial, E.at[0]))
    for a, (ref, A) in enumerate(arriving):
        for n in (4, 3, 5, 2, 6, 1, 7, 0):
            jj = (j + n) % RING
            src = ref.at[:, pl.ds(pl.multiple_of(jj * 8, 8), 8), :]
            dst = A.at[zs, 0, c]
            if n == 0:
                @pl.when(stay)
                def _():
                    pltpu.make_async_copy(src, dst, crecv.at[a]).start()

                @pl.when(jnp.logical_not(stay))
                def _():
                    remote(src, dst, csend, crecv.at[a], (snake(q) * RING + j, half)).start()
            else:
                remote(src, dst, csend, crecv.at[a], (snake(q) * RING + jj, half)).start()

    send_forcing(1, 16)

    @pl.when(q < 4)
    def _():
        send_forcing(16, 2 * COLS)

    for a, (ref, A) in enumerate(arriving):
        await_bytes(forcing.at[0, pl.ds(0, 32)], crecv.at[a])
        if a < 2:
            halo_copies(A, xsend.at[a], xrecv.at[a], 3)
        else:
            halo_copies(A, hsend.at[0], hrecv.at[0], 4)

    @pl.when(q >= 4)
    def _():
        send_forcing(16, 2 * COLS)

    await_halos(xrecv.at[0], 3)
    await_halos(xrecv.at[1], 3)
    for z in range(0, 24, 4):
        s = pl.ds(z, 4)
        d, r = D[s], R[s]
        inv = 1.0 / (1.0 + 6.0 * d + r)
        IV[s] = inv
        DP[s] = d * inv
        EP[s] = (d + r) * inv
    for A in (IV, DP, EP):
        clear_outside(A)

    def send_force(k):
        halo_copies(G.at[k], gsend.at[k], grecv.at[k], 3)

    def await_force(k):
        await_bytes(forcing.at[0, pl.ds(0, 32)], frecv.at[k])

    await_force(0)
    send_force(0)

    def relax(load, load_s, z, n, tiles):
        shape = (n, 8, 128)
        row = lax.broadcasted_iota(jnp.int32, shape, 1)
        lane = lax.broadcasted_iota(jnp.int32, shape, 2)
        first_row, last_row = row == 0, row == 7
        first_lane, last_lane = lane == 0, lane == 127
        zero = jnp.zeros(shape, F32)
        wide = [[load(z - 1, n + 2, T, h) for h in range(2)] for T in range(tiles)]
        mid = [[wide[T][h][1:-1] for h in range(2)] for T in range(tiles)]
        if tiles == 1:
            mid.append([load(z, n, 1, h) for h in range(2)])
        result = [[None, None] for T in range(tiles)]
        beside = [[None, None] for T in range(tiles)]
        for h in range(2):
            a = [pltpu.roll(mid[T][h], 1, 1) for T in range(2)]
            b = [pltpu.roll(mid[T][h], 7, 1) for T in range(2)]
            for T in range(tiles):
                beside[T][h] = jnp.where(first_row, a[1 - T], a[T]) + jnp.where(last_row, b[1 - T], b[T])
        for T in range(tiles):
            a0, a1 = pltpu.roll(mid[T][0], 1, 2), pltpu.roll(mid[T][1], 1, 2)
            b0, b1 = pltpu.roll(mid[T][0], 127, 2), pltpu.roll(mid[T][1], 127, 2)
            across = (
                jnp.where(first_lane, zero, a0) + jnp.where(last_lane, b1, b0),
                jnp.where(first_lane, a0, a1) + jnp.where(last_lane, zero, b1),
            )
            for h in range(2):
                total = beside[T][h] + across[h] + wide[T][h][2:]
                s = pl.ds(z, n)
                result[T][h] = (
                    load_s(z, n, T, h) + DP[s, T, h] * total + EP[s, T, h] * wide[T][h][:-2]
                )
        return result

    def chunks(first, last):
        z = first
        while z < last:
            n = min(4, last - z)
            yield z, n
            z += n

    def from_ref(A):
        return lambda z, n, T, h: A[pl.ds(z, n), T, h]

    def send_state(k, piece):
        rows = 16 // PIECES
        for h in range(2):
            src = E.at[k + 1, pl.ds(4 + piece * rows, rows), 0, h]
            dst = out.at[0, pl.ds(part * 16 + piece * rows, rows)]
            mine = jnp.logical_and(k == q, c == h)

            @pl.when(mine)
            def _():
                pltpu.make_async_copy(src, dst, orecv).start()

            @pl.when(jnp.logical_not(mine))
            def _():
                remote(src, dst, osend, orecv, (k * RING + j, h)).start()

    @pl.loop(0, NT)
    def _(k):
        now, later = E.at[k], E.at[k + 1]
        force = G.at[k]
        await_halos(grecv.at[k], 3)
        await_halos(hrecv.at[k], 4)

        def make_source(z, n, T, h):
            s = pl.ds(z, n)
            v = (now[s, T, h] + force[s, T, h]) * IV[s, T, h]
            SP[s, T, h] = v
            return v

        for load, load_s, W, margin in (
            (from_ref(now), make_source, W1, 1),
            (from_ref(W1), from_ref(SP), W2, 2),
            (from_ref(W2), from_ref(SP), W1, 3),
        ):
            for z, n in chunks(margin, 24 - margin):
                v = relax(load, load_s, z, n, 2)
                for T in range(2):
                    for h in range(2):
                        W[pl.ds(z, n), T, h] = v[T][h]

        for z, n in ((4, 4), (16, 4), (8, 4), (12, 4)):
            if z == 8:
                @pl.when(k < NT - 1)
                def _():
                    halo_copies(later, hsend.at[k + 1], hrecv.at[k + 1], 4, 0)

            v = relax(from_ref(W1), from_ref(SP), z, n, 1)
            for h in range(2):
                later[pl.ds(z, n), 0, h] = v[0][h]

        @pl.when(k < NT - 1)
        def _():
            halo_copies(later, hsend.at[k + 1], hrecv.at[k + 1], 4, 1)

        for d in range(PIECES):
            @pl.when(k >= d)
            def _():
                send_state(k - d, d)

        @pl.when(k == 0)
        def _():
            await_halos(hsend.at[0], 4)
            await_force(1)

        @pl.when(k < NT - 2)
        def _():
            await_force(k + 2)

        @pl.when(k < NT - 1)
        def _():
            await_halos(hsend.at[k + 1], 4)

        @pl.when(k == 0)
        def _():
            send_force(1)

        @pl.when(k < NT - 2)
        def _():
            send_force(k + 2)

    for k in range(NT - PIECES + 1, NT):
        for piece in range(NT - k, PIECES):
            send_state(k, piece)

    @pl.when(stay)
    def _():
        await_bytes(forcing.at[0, pl.ds(0, 84)], csend)

    @pl.when(jnp.logical_not(stay))
    def _():
        await_bytes(forcing.at[0, pl.ds(0, 96)], csend)

    await_halos(xsend.at[0], 3)
    await_halos(xsend.at[1], 3)

    @pl.loop(0, NT)
    def _(k):
        await_halos(gsend.at[k], 3)

    await_bytes(forcing.at[0, pl.ds(0, 496)], fsend)
    await_bytes(forcing.at[0, pl.ds(0, 496)], osend)
    await_bytes(out, orecv)


def per_device(forcing, initial, diffusion, drift):
    wide = (24, 2, 2, 8, 128)
    vmem = lambda *shape: pltpu.VMEM(shape, F32)
    dma = pltpu.SemaphoreType.DMA
    return pl.pallas_call(
        kernel,
        out_shape=jax.ShapeDtypeStruct(forcing.shape, F32),
        in_specs=[pl.BlockSpec(memory_space=pltpu.HBM)] * 4,
        out_specs=pl.BlockSpec(memory_space=pl.ANY),
        scratch_shapes=[vmem(NT, *wide), vmem(NT + 1, *wide)]
        + [vmem(*wide)] * 8
        + [dma, dma((3,)), dma((2, 3)), dma((2, 3)), dma, dma((NT,)), dma((NT, 3)), dma((NT, 3))]
        + [dma((NT, 3)), dma((NT, 3)), dma, dma],
        compiler_params=pltpu.CompilerParams(
            collective_id=0, has_side_effects=True, vmem_limit_bytes=40 * 1024 * 1024
        ),
    )(*[pltpu.with_memory_space_constraint(a, pltpu.HBM) for a in (forcing, initial, diffusion, drift)])


def solution(mesh):
    in_specs = (
        P("tm", None, None, "space"),
        P("tm", None, "space"),
        P("tm", None, "space"),
        P("tm", None, "space"),
    )
    out_specs = P("tm", None, None, "space")
    return jax.shard_map(
        per_device, mesh=mesh, in_specs=in_specs, out_specs=out_specs, check_vma=False
    )
```
